32 devices in a mesh: groups: 2 (over x), ctx: 16 (over z, y, core).
Axes of the slice: x: 2, y: 2, z: 4, core: 2. Of those that a mesh axis runs over, the one named last changes fastest.
Arguments:
- queries: bfloat16 [4096, 2048], P(('groups', 'ctx')), parts along dimension 0, may hold values from -64 to 64
- keys: bfloat16 [4096, 512], P(('groups', 'ctx')), parts along dimension 0, may hold values from -6 to 6
- values: bfloat16 [4096, 512], P(('groups', 'ctx')), parts along dimension 0, may hold values from -6 to 6
- block_ids: int32 [4096], P(('groups', 'ctx')), parts along dimension 0, may hold values from 0 to 3, as said below
- out_weight: bfloat16 [2048, 2048], P('ctx'), may hold values from -0.59765625 to 0.59765625
- summary_gain: float32 [128], replicated, may hold values from 0.1 to 1.9
- norm_gain: float32 [2048], replicated, may hold values from 0.1 to 1.9
- routes: int32 [4096, 8], P(('groups', 'ctx')), parts along dimension 0, may hold values from 0 to 15, all different within a row; in each aligned block of 128 rows (0 to 127, 128 to 255, ...) at most 80 rows name the same one
- route_scores: float32 [4096, 8], P(('groups', 'ctx')), parts along dimension 0, may hold values from 0.02 to 1
- expert_gate: bfloat16 [16, 2048, 768], P('ctx'), may hold values from -0.125 to 0.125
- expert_up: bfloat16 [16, 2048, 768], P('ctx'), may hold values from -0.125 to 0.125
- expert_down: bfloat16 [16, 768, 2048], P('ctx'), may hold values from -0.21875 to 0.21875
Outputs:
- projected: bfloat16 [4096, 2048], P(('groups', 'ctx')), parts along dimension 0
- mixed: bfloat16 [4096, 2048], P(('groups', 'ctx')), parts along dimension 0
The draws below stay inside these ranges and needn't reach their ends.
There are 2 independent parts, one for each index of `groups`. The reference program is written for one: setup_inputs(seed, part) draws one part's arguments, and reference() takes and returns one part's arrays. A program takes and returns all parts, laid end to end along the dimension named above; an argument that names none is the same for every part. Nothing has to cross between parts.
Inputs may be any that keep to these rules, and one draw needn't show every extreme that they name: `block_ids`: within each context shard's 128 tokens the block numbers never fall, start at 0 and take every value up to 3. `routes`: among the 128 tokens of one context shard no expert is chosen more than 80 times, and in every draw some expert is chosen exactly 80 times by some shard. A token's 8 experts differ.
All inputs are finite; a program needn't handle non-finite values.
Results may differ from the reference program's by a relative error of at most 0.0077.
Values may be sent and summed in bfloat16 or wider, within the bound.
A program may use at most 128 MiB of HBM per device.

```python
import math
import jax
import jax.numpy as jnp
import numpy as np
from jax import lax

D = 2048
HQ = 16
KVH = 4
HD = 128
FF = 768
TOP = 8
NB = 4
TOK_DEV = 128
TOKENS = 2048
EXPERTS = 16
CAP = 80


def query_key_pair(key):
    key_q = jax.random.fold_in(key, 101)
    key_k = jax.random.fold_in(key, 202)
    query = jax.random.truncated_normal(key_q, -6.0, 6.0, (TOKENS, HQ * HD), jnp.float32)
    keyed = jax.random.truncated_normal(key_k, -6.0, 6.0, (TOKENS, KVH * HD), jnp.float32)
    return (query, keyed)


def draw_queries(key, part):
    return query_key_pair(key)[0].astype(jnp.bfloat16)


def draw_keys(key, part):
    return query_key_pair(key)[1].astype(jnp.bfloat16)


def draw_block_ids(key, part):
    shards = TOKENS // TOK_DEV
    subkeys = jax.random.split(jax.random.fold_in(key, 303), shards)

    def one_shard(sub):
        cuts = jax.random.permutation(sub, TOK_DEV - 1)[:NB - 1] + 1
        position = jnp.arange(TOK_DEV)
        return jnp.sum((position[:, None] >= cuts[None, :]).astype(jnp.int32), axis=-1)
    return jax.vmap(one_shard)(subkeys).reshape(TOKENS).astype(jnp.int32)


def level_of(rng, shape, cuts, smallest, top_value):
    level = 1.0
    for dim, parts in cuts:
        heights = jax.random.uniform(jax.random.fold_in(jax.random.fold_in(rng, 6), dim), (parts,), jnp.float32, smallest / len(cuts), top_value / len(cuts))
        level = level * jnp.repeat(jnp.exp(heights), shape[dim] // parts).reshape((-1,) + (1,) * (len(shape) - 1 - dim))
    return level


def deal_out(stream_key, own, number, rows, number_of, top, most, slope):
    order = jax.random.permutation(stream_key, number_of)
    crowded, common = portions_of(number_of, rows * top, most, slope, True), portions_of(number_of, rows * top, most, slope, False)
    places = jnp.arange(number_of)

    def named(lengths, turn):
        used = int((lengths > 0).sum())
        fixed = max(1, used // 4)
        moved = fixed + (places - fixed + turn * (used - fixed)) % max(1, number_of - fixed)
        return jnp.zeros((number_of,), jnp.int32).at[order[jnp.where(places < fixed, places, moved)]].set(jnp.asarray(lengths, jnp.int32))

    lengths = jnp.where(number % 4 == 0, named(crowded, number // 4), named(common, number - number // 4 - 1))
    mixed = jax.random.permutation(jax.random.fold_in(own, 3), number_of)
    giver, sink = mixed[0:number_of // 2 * 2:2], mixed[1:number_of // 2 * 2:2]
    room = jnp.minimum(lengths[giver] - 1, most - lengths[sink]) // 2
    room = jnp.where((giver == order[0]) | (sink == order[0]) | (lengths[sink] == 0), 0, jnp.maximum(room, 0))
    moved = jax.random.randint(jax.random.fold_in(own, 4), (number_of // 2,), 0, 1 << 20) % (room + 1)
    lengths = lengths.at[giver].add(-moved).at[sink].add(moved)
    members = jnp.searchsorted(jnp.cumsum(lengths), jnp.arange(rows * top), side="right").astype(jnp.int32)
    listing = members.reshape(top, rows).T
    listing = listing[jax.random.permutation(jax.random.fold_in(own, 1), rows)]
    turn = jax.random.randint(jax.random.fold_in(own, 2), (rows, 1), 0, top)
    return jnp.take_along_axis(listing, (jnp.arange(top)[None, :] + turn) % top, axis=1)


def portions_of(count, total, limit, lean, full):
    portions = [(1 << 20) // math.isqrt(rank ** lean) + 1 for rank in range(1, count + 1)]
    largest = limit if full else min(limit, max(-(-total // count), total * portions[0] // sum(portions)))
    least = 1 if total - largest >= count - 1 else 0
    holding, spare = [largest] + [least] * (count - 1), total - largest - least * (count - 1)
    while spare > 0:
        free = [i for i in range(1, count) if holding[i] < largest] or [i for i in range(1, count) if holding[i] < limit]
        mass, budget = sum([portions[i] for i in free]), spare
        for i in free:
            more = min(limit - holding[i], max(1, budget * portions[i] // mass), spare)
            holding[i] = holding[i] + more
            spare = spare - more
    return np.array(holding)


def scatter_about(own_key, dims, spread, limit, pieces=(), held_as=jnp.bfloat16):
    array = jax.random.normal(own_key, dims, jnp.float32) * spread
    if len(pieces) > 0:
        array = level_of(own_key, dims, pieces, -0.22, 0.18) * array
    return jnp.clip(array, min=-limit, max=limit).astype(held_as)


def setup_inputs(seed: int = 0, part: int = 0) -> dict:
    seeds = jax.random.split(jax.random.key(seed), 13)
    part_splits = jax.random.split(jax.random.fold_in(seeds[12], part), 13)
    queries = draw_queries(jax.random.fold_in(jax.random.fold_in(seeds[12], part), 71), part)
    keys = draw_keys(jax.random.fold_in(jax.random.fold_in(seeds[12], part), 71), part)
    values = scatter_about(part_splits[2], (TOKENS, KVH * HD), 1.0, 6.0, ((0, 16),))
    block_ids = draw_block_ids(jax.random.fold_in(jax.random.fold_in(seeds[12], part), 71), part)
    out_weight = scatter_about(seeds[4], (HQ * HD, D), 0.1, 0.59765625, ((0, 16),))
    summary_gain = jnp.clip(1.0 + 0.18 * jax.random.normal(seeds[5], (HD,), jnp.float32), 0.1, 1.9)
    norm_gain = jnp.clip(1.0 + 0.18 * jax.random.normal(seeds[6], (D,), jnp.float32), 0.1, 1.9)
    routes_keys = jax.random.split(jax.random.fold_in(part_splits[7], 1), TOKENS // TOK_DEV)
    routes_turns = jax.random.permutation(jax.random.fold_in(part_splits[7], 3), TOKENS // TOK_DEV)
    routes = jax.vmap(lambda own, number: deal_out(jax.random.fold_in(part_splits[7], 2), own, number, TOK_DEV, EXPERTS, TOP, CAP, 2))(routes_keys, routes_turns).reshape((TOKENS, TOP))
    route_scores = jnp.clip(jnp.exp(math.log(1.0) - 3.912023 * jax.random.uniform(part_splits[8], (TOKENS, TOP), jnp.float32) ** level_of(part_splits[8], (TOKENS, TOP), ((0, 16),), -0.2, 0.2)), 0.02, 1.0)
    expert_gate = scatter_about(seeds[9], (EXPERTS, D, FF), D ** -0.5, 0.125, ((0, 16),))
    expert_up = scatter_about(seeds[10], (EXPERTS, D, FF), D ** -0.5, 0.125, ((0, 16),))
    expert_down = scatter_about(seeds[11], (EXPERTS, FF, D), FF ** -0.5, 0.21875, ((0, 16),))
    return {"queries": queries, "keys": keys, "values": values, "block_ids": block_ids, "out_weight": out_weight, "summary_gain": summary_gain, "norm_gain": norm_gain, "routes": routes, "route_scores": route_scores, "expert_gate": expert_gate, "expert_up": expert_up, "expert_down": expert_down}


def normalize(x):
    return x * lax.rsqrt(lax.optimization_barrier(jnp.mean(x * x, axis=-1, keepdims=True)) + 1e-06)

def reference(queries, keys, values, block_ids, out_weight, summary_gain, norm_gain, routes, route_scores, expert_gate, expert_up, expert_down):
    shards = TOKENS // TOK_DEV
    group = HQ // KVH
    scale = 1.0 / math.sqrt(HD)
    keys4 = keys.astype(jnp.float32).reshape(shards, TOK_DEV, KVH, HD)
    values4 = values.astype(jnp.float32).reshape(shards, TOK_DEV, KVH, HD)
    blocks = block_ids.reshape(shards, TOK_DEV)
    member = (blocks[:, None, :] == jnp.arange(NB, dtype=jnp.int32)[None, :, None]).astype(jnp.float32)
    count = lax.optimization_barrier(jnp.sum(member, axis=-1))
    kmean = jnp.einsum('nbt,ntkd->nbkd', member, keys4) / count[:, :, None, None]
    vmean = jnp.einsum('nbt,ntkd->nbkd', member, values4) / count[:, :, None, None]
    summary_keys = (normalize(kmean) * summary_gain.astype(jnp.float32)).astype(jnp.bfloat16).reshape(shards * NB, KVH, HD)
    summary_values = normalize(vmean).astype(jnp.bfloat16).reshape(shards * NB, KVH, HD)
    owner = jnp.arange(shards * NB, dtype=jnp.int32) // NB
    causal = jnp.arange(TOK_DEV)[:, None] >= jnp.arange(TOK_DEV)[None, :]

    def attend(index):
        start = (index * TOK_DEV).astype(jnp.int32)
        query = lax.dynamic_slice_in_dim(queries, start, TOK_DEV, 0).astype(jnp.float32).reshape(TOK_DEV, KVH, group, HD)
        key_loc = lax.dynamic_slice_in_dim(keys, start, TOK_DEV, 0).astype(jnp.float32).reshape(TOK_DEV, KVH, HD)
        val_loc = lax.dynamic_slice_in_dim(values, start, TOK_DEV, 0).reshape(TOK_DEV, KVH, HD)
        local = jnp.einsum('tkgd,skd->kgts', query, key_loc) * scale
        local = jnp.where(causal[None, None], local, -jnp.inf)
        remote = jnp.einsum('tkgd,skd->kgts', query, summary_keys.astype(jnp.float32)) * scale
        remote = jnp.where((owner < index)[None, None, None, :], remote, -jnp.inf)
        scores = jnp.concatenate([local, remote], axis=-1)
        top = lax.optimization_barrier(jnp.max(scores, axis=-1, keepdims=True))
        expo = jnp.exp(scores - top)
        weights = (expo / lax.optimization_barrier(jnp.sum(expo, axis=-1, keepdims=True))).astype(jnp.bfloat16)
        every_value = jnp.concatenate([val_loc, summary_values], axis=0)
        out = jnp.einsum('kgts,skd->tkgd', weights.astype(jnp.float32), every_value.astype(jnp.float32))
        return out.reshape(TOK_DEV, HQ * HD).astype(jnp.bfloat16)
    attended = lax.map(attend, jnp.arange(shards, dtype=jnp.int32)).reshape(TOKENS, HQ * HD)
    hidden = jnp.dot(attended, out_weight, preferred_element_type=jnp.float32)
    normed = (normalize(hidden) * norm_gain.astype(jnp.float32)).astype(jnp.bfloat16)
    combine = route_scores / lax.optimization_barrier(jnp.sum(route_scores, axis=-1, keepdims=True))
    slots = shards * CAP

    def expert_step(total, expert):
        picked = routes == expert
        weight_tok = lax.optimization_barrier(jnp.sum(jnp.where(picked, combine, 0.0), axis=-1))
        chosen = jnp.any(picked, axis=-1)
        rows = jnp.nonzero(chosen, size=slots, fill_value=0)[0].astype(jnp.int32)
        used = jnp.arange(slots) < jnp.sum(chosen.astype(jnp.int32))
        inputs = normed[rows]
        gate = jnp.dot(inputs, expert_gate[expert], preferred_element_type=jnp.float32)
        upper = jnp.dot(inputs, expert_up[expert], preferred_element_type=jnp.float32)
        act = (jax.nn.silu(gate) * upper).astype(jnp.bfloat16)
        result = jnp.dot(act, expert_down[expert], preferred_element_type=jnp.float32).astype(jnp.bfloat16)
        contrib = jnp.where(used[:, None], weight_tok[rows][:, None] * result.astype(jnp.float32), 0.0)
        return (total.at[rows].add(contrib), None)
    total, _ = lax.scan(expert_step, jnp.zeros((TOKENS, D), jnp.float32), jnp.arange(EXPERTS, dtype=jnp.int32))
    return (hidden.astype(jnp.bfloat16), (hidden + total).astype(jnp.bfloat16))
```

```python
import functools
import math

import jax
import jax.numpy as jnp
from jax import lax
from jax.experimental import pallas as pl
from jax.experimental.pallas import tpu as pltpu
from jax.sharding import PartitionSpec as P

D = 2048
HQ = 16
KVH = 4
HD = 128
TOP = 8
EXP_DEV = 1
NB = 4


def normalize(x):
    return x * lax.rsqrt(jnp.mean(x * x, axis=-1, keepdims=True) + 1e-06)


RING_BYTES = 16 * 2**20


def chip_at(position, chips):
    depth = chips // 2
    y = position // depth
    return (position * (1 - y) + (chips - 1 - position) * y) * 2 + y


def moe_kernel(
    n,
    cap,
    normed,
    hidden,
    share,
    gate_hbm,
    up_hbm,
    down_hbm,
    out,
    gate_w,
    up_w,
    down_w,
    tok,
    wbuf,
    rows_in,
    act,
    place,
    comb,
    mine,
    outgo,
    theirs,
    ring_in,
    load_sem,
    own_sem,
    w_send,
    w_recv,
    ag_send,
    ag_recv,
    pt_send,
    pt_recv,
    y_send,
    y_recv,
    rs_send_sem,
    rs_recv_sem,
):
    tokens = normed.shape[0]
    half = tokens // 2
    width = normed.shape[1]
    ff = gate_w.shape[1]
    chips = n // 2
    far = chips // 2
    me = lax.axis_index("ctx")
    core = me % 2
    y = (me // 2) % 2
    z = me // 4
    pos = z * (1 - y) + (chips - 1 - z) * y
    partner = me + 1 - 2 * core
    ahead = chip_at((pos + 1) % chips, chips) * 2 + core
    behind = chip_at((pos + chips - 1) % chips, chips) * 2 + core
    neighbour = (ahead, behind)

    loads = [
        pltpu.make_async_copy(a, b, load_sem.at[k])
        for k, (a, b) in enumerate(((gate_hbm, gate_w), (up_hbm, up_w), (down_hbm, down_w)))
    ]
    for load in loads:
        load.start()
    own = pltpu.make_async_copy(normed, tok.at[pos, core], own_sem)
    own.start()

    barrier = pltpu.get_barrier_semaphore()

    def greet(k, _):
        pl.semaphore_signal(barrier, inc=1, device_id={"ctx": (me + k) % n})
        return 0

    lax.fori_loop(1, n, greet, 0)
    pl.semaphore_wait(barrier, n - 1)

    def rows(h):
        return pl.ds(h * half, half)

    def chip(offset):
        return (pos + offset + chips) % chips

    def ag_copy(d, step, h):
        sign = 1 - 2 * d
        q = chip(-sign * (step - 1))
        src = normed.at[rows(h)] if step == 1 else tok.at[q, core, rows(h)]
        return pltpu.make_async_remote_copy(
            src_ref=src,
            dst_ref=tok.at[q, core, rows(h)],
            send_sem=ag_send.at[d, step - 1, h],
            recv_sem=ag_recv.at[d, step - 1, h],
            device_id={"ctx": neighbour[d]},
        )

    def pt_copy(offset, h):
        q = chip(offset)
        src = normed.at[rows(h)] if offset == 0 else tok.at[q, core, rows(h)]
        return pltpu.make_async_remote_copy(
            src_ref=src,
            dst_ref=tok.at[q, core, rows(h)],
            send_sem=pt_send.at[offset % chips, h],
            recv_sem=pt_recv.at[offset % chips, h],
            device_id={"ctx": partner},
        )

    def order(d):
        return (0, 1) if d == 0 else (1, 0)

    for k in range(2):
        for d in range(2):
            ag_copy(d, 1, order(d)[k]).start()
    for h in range(2):
        pt_copy(0, h).start()

    def w_copy(k):
        target = (me + k) % n
        return pltpu.make_async_remote_copy(
            src_ref=share.at[target],
            dst_ref=wbuf.at[pos * 2 + core],
            send_sem=w_send.at[k],
            recv_sem=w_recv.at[k],
            device_id={"ctx": target},
        )

    def w_start(k, _):
        w_copy(k).start()
        return 0

    def w_wait(k, _):
        w_copy(k).wait()
        return 0

    lax.fori_loop(1, n, w_start, 0)
    wbuf[pos * 2 + core] = share[me]
    own.wait()
    lax.fori_loop(1, n, w_wait, 0)
    for load in loads:
        load.wait()

    def y_copy(offset):
        q = chip(offset)
        return pltpu.make_async_remote_copy(
            src_ref=outgo.at[q],
            dst_ref=theirs.at[q],
            send_sem=y_send.at[offset % chips],
            recv_sem=y_recv.at[offset % chips],
            device_id={"ctx": partner},
        )

    def compute(offset):
        q = chip(offset)
        for h in range(2):
            pt_copy(offset, h).wait_recv()
        earlier = lax.broadcasted_iota(jnp.int32, (tokens, tokens), 0) < lax.broadcasted_iota(
            jnp.int32, (tokens, tokens), 1
        )
        earlier = jnp.where(earlier, 1.0, 0.0).astype(jnp.bfloat16)
        line = lax.broadcasted_iota(jnp.int32, (cap, tokens), 0).astype(jnp.float32)
        for rel in range(2):
            side = (core + rel) % 2
            weight = wbuf[q * 2 + side]
            chosen = jnp.where(weight > 0.0, 1.0, 0.0)
            slot = jnp.dot(chosen.astype(jnp.bfloat16), earlier, preferred_element_type=jnp.float32)
            slot = jnp.where(weight > 0.0, slot, -1.0)
            hit = jnp.broadcast_to(slot[0:1], (cap, tokens)) == line
            pick = jnp.where(hit, 1.0, 0.0).astype(jnp.bfloat16)
            place[rel] = pick
            scaled = jnp.where(hit, jnp.broadcast_to(weight[0:1], (cap, tokens)), 0.0)
            comb[rel] = jnp.broadcast_to(jnp.sum(scaled, axis=1, keepdims=True), (cap, 128))
            for c in range(0, width, 512):
                rows_in[rel * cap : (rel + 1) * cap, c : c + 512] = jnp.dot(
                    pick, tok[q, side, :, c : c + 512], preferred_element_type=jnp.float32
                ).astype(jnp.bfloat16)

        def in_tile(k, _):
            cols = pl.ds(pl.multiple_of(k * 256, 256), 256)
            x = rows_in[...]
            g = jnp.dot(x, gate_w[:, cols], preferred_element_type=jnp.float32)
            u = jnp.dot(x, up_w[:, cols], preferred_element_type=jnp.float32)
            act[:, cols] = (g / (1.0 + jnp.exp(-g)) * u).astype(jnp.bfloat16)
            return 0

        lax.fori_loop(0, ff // 256, in_tile, 0)

        def out_tile(k, _):
            cols = pl.ds(pl.multiple_of(k * 512, 512), 512)
            r = jnp.dot(act[...], down_w[:, cols], preferred_element_type=jnp.float32)
            r = r.astype(jnp.bfloat16).astype(jnp.float32)
            for rel, dest in ((0, mine), (1, outgo)):
                part = r[rel * cap : (rel + 1) * cap] * comb[rel][:, 0:1]
                dest[q, :, cols] = lax.dot_general(
                    place[rel],
                    part.astype(jnp.bfloat16),
                    (((0,), (0,)), ((), ())),
                    preferred_element_type=jnp.float32,
                ).astype(jnp.bfloat16)
            return 0

        lax.fori_loop(0, width // 512, out_tile, 0)
        y_copy(offset).start()

    for step in range(1, far):
        for k in range(2):
            for d in range(2):
                h = order(d)[k]
                sign = 1 - 2 * d
                ag_copy(d, step, h).wait_recv()
                if step + 1 < far or k == 0:
                    ag_copy(d, step + 1, h).start()
                pt_copy(-sign * step, h).start()
            if step == 1:
                if k == 0:
                    compute(0)
            else:
                compute((step - 1) * (2 * k - 1))
    compute(1 - far)
    compute(far - 1)
    for d in range(2):
        h = order(d)[0]
        ag_copy(d, far, h).wait_recv()
        pt_copy(far, h).start()

    def sum_of(q, h):
        return mine[q, rows(h)].astype(jnp.float32) + theirs[q, rows(h)].astype(jnp.float32)

    def rs_copy(d, step, h, src):
        return pltpu.make_async_remote_copy(
            src_ref=src,
            dst_ref=ring_in.at[d, step - 1, h],
            send_sem=rs_send_sem.at[d, step - 1, h],
            recv_sem=rs_recv_sem.at[d, step - 1, h],
            device_id={"ctx": neighbour[d]},
        )

    def rs_step(d, step, k):
        h = order(d)[k]
        sign = 1 - 2 * d
        q = chip(sign * (far + 1 - step))
        if step == 1 or (step == 2 and k == 1):
            mine[q, rows(h)] = sum_of(q, h).astype(jnp.bfloat16)
            src = mine.at[q, rows(h)]
        else:
            src = ring_in.at[d, step - 2, h]
            rs_copy(d, step - 1, h, src).wait_recv()
            ring_in[d, step - 2, h] = (
                ring_in[d, step - 2, h].astype(jnp.float32) + sum_of(q, h)
            ).astype(jnp.bfloat16)
        rs_copy(d, step, h, src).start()

    for offset in range(chips):
        if offset != far:
            y_copy(offset).wait_recv()
    for d in range(2):
        rs_step(d, 2, 1)
    compute(far)
    y_copy(far).wait_recv()
    sends = [(1, 0)]
    for step in range(2, far + 1):
        if step < far:
            sends += [(step + 1, 1)]
        sends += [(step, 0)]
    for step, k in sends:
        for d in range(2):
            rs_step(d, step, k)
    for h in range(2):
        total = hidden[rows(h)] + sum_of(pos, h)
        for d in range(2):
            rs_copy(d, far, h, ring_in.at[d, far - 1, h]).wait_recv()
            total = total + ring_in[d, far - 1, h].astype(jnp.float32)
        out[rows(h)] = total.astype(jnp.bfloat16)

    for d in range(2):
        for step in range(1, far + 1):
            for k in range(2):
                h = order(d)[k]
                if step < far or k == 0:
                    ag_copy(d, step, h).wait_send()
                if step > 1 or k == 0:
                    rs_copy(d, step, h, ring_in.at[d, step - 1, h]).wait_send()
    for offset in range(chips):
        for h in range(2):
            pt_copy(offset, h).wait_send()
        y_copy(offset).wait_send()


def moe_ring(normed, hidden, share, expert_gate, expert_up, expert_down, n, cap):
    tokens, width = normed.shape
    ff = expert_gate.shape[-1]
    chips = n // 2
    far = chips // 2
    vmem = pl.BlockSpec(memory_space=pltpu.VMEM)
    hbm = pl.BlockSpec(memory_space=pl.ANY)
    dma = pltpu.SemaphoreType.DMA
    bf16 = jnp.bfloat16
    return pl.pallas_call(
        functools.partial(moe_kernel, n, cap),
        out_shape=jax.ShapeDtypeStruct((tokens, width), bf16),
        in_specs=[vmem, vmem, vmem, hbm, hbm, hbm],
        out_specs=vmem,
        scratch_shapes=[
            pltpu.VMEM((width, ff), bf16),
            pltpu.VMEM((width, ff), bf16),
            pltpu.VMEM((ff, width), bf16),
            pltpu.VMEM((chips, 2, tokens, width), bf16),
            pltpu.VMEM((n, 8, tokens), jnp.float32),
            pltpu.VMEM((2 * cap, width), bf16),
            pltpu.VMEM((2 * cap, ff), bf16),
            pltpu.VMEM((2, cap, tokens), bf16),
            pltpu.VMEM((2, cap, 128), jnp.float32),
            pltpu.VMEM((chips, tokens, width), bf16),
            pltpu.VMEM((chips, tokens, width), bf16),
            pltpu.VMEM((chips, tokens, width), bf16),
            pltpu.VMEM((2, far, 2, tokens // 2, width), bf16),
            dma((3,)),
            dma,
            dma((n,)),
            dma((n,)),
            dma((2, far, 2)),
            dma((2, far, 2)),
            dma((chips, 2)),
            dma((chips, 2)),
            dma((chips,)),
            dma((chips,)),
            dma((2, far, 2)),
            dma((2, far, 2)),
        ],
        compiler_params=pltpu.CompilerParams(
            collective_id=1, has_side_effects=True, vmem_limit_bytes=60 * 2**20
        ),
    )(normed, hidden, share, expert_gate[0], expert_up[0], expert_down[0])


def body(
    queries,
    keys,
    values,
    block_ids,
    out_weight,
    summary_gain,
    norm_gain,
    routes,
    route_scores,
    expert_gate,
    expert_up,
    expert_down,
):
    tokens_here = queries.shape[0]
    group = HQ // KVH
    scale = 1.0 / math.sqrt(HD)
    member = block_ids[None, :] == jnp.arange(NB, dtype=jnp.int32)[:, None]
    count = jnp.sum(member.astype(jnp.float32), axis=-1)
    indicator = member.astype(jnp.bfloat16)
    kmean = jnp.dot(indicator, keys, preferred_element_type=jnp.float32) / count[:, None]
    vmean = jnp.dot(indicator, values, preferred_element_type=jnp.float32) / count[:, None]
    summary_keys = (
        (normalize(kmean.reshape(NB, KVH, HD)) * summary_gain)
        .astype(jnp.bfloat16)
        .reshape(NB, KVH * HD)
    )
    summary_values = (
        normalize(vmean.reshape(NB, KVH, HD)).astype(jnp.bfloat16).reshape(NB, KVH * HD)
    )
    summaries = lax.all_gather(
        jnp.concatenate([summary_keys, summary_values], axis=1), "ctx", axis=0, tiled=True
    )
    all_keys, all_values = summaries[:, : KVH * HD], summaries[:, KVH * HD :]
    index = lax.axis_index("ctx")
    query = queries.reshape(tokens_here, KVH, group, HD)
    key_loc = keys.reshape(tokens_here, KVH, HD)
    remote_keys = all_keys.reshape(-1, KVH, HD)
    causal = jnp.arange(tokens_here)[:, None] >= jnp.arange(tokens_here)[None, :]
    owner = jnp.arange(remote_keys.shape[0], dtype=jnp.int32) // NB
    local = jnp.einsum("tkgd,skd->kgts", query, key_loc, preferred_element_type=jnp.float32) * scale
    local = jnp.where(causal[None, None], local, -jnp.inf)
    remote = (
        jnp.einsum("tkgd,skd->kgts", query, remote_keys, preferred_element_type=jnp.float32) * scale
    )
    remote = jnp.where((owner < index)[None, None, None, :], remote, -jnp.inf)
    scores = jnp.concatenate([local, remote], axis=-1)
    top = jnp.max(scores, axis=-1, keepdims=True)
    expo = jnp.exp(scores - top)
    weights = (expo / jnp.sum(expo, axis=-1, keepdims=True)).astype(jnp.bfloat16)
    every_value = jnp.concatenate(
        [values.reshape(tokens_here, KVH, HD), all_values.reshape(-1, KVH, HD)], axis=0
    )
    attended = jnp.einsum(
        "kgts,skd->tkgd", weights, every_value, preferred_element_type=jnp.float32
    )
    attended = attended.reshape(tokens_here, HQ * HD).astype(jnp.bfloat16)
    hidden = jnp.dot(
        attended,
        lax.all_gather(out_weight, "ctx", axis=0, tiled=True),
        preferred_element_type=jnp.float32,
    )
    normed = (normalize(hidden) * norm_gain).astype(jnp.bfloat16)
    combine = route_scores / jnp.sum(route_scores, axis=-1, keepdims=True)
    experts_all = EXP_DEV * lax.axis_size("ctx")
    capacity = max(2, 5 * tokens_here * TOP // (4 * experts_all))
    chips = experts_all // 2
    if chips % 4 == 0 and experts_all * tokens_here * D * 2 <= RING_BYTES:
        named = routes[:, :, None] == jnp.arange(experts_all, dtype=jnp.int32)[None, None, :]
        share = jnp.sum(jnp.where(named, combine[:, :, None], 0.0), axis=1).T
        share = jnp.broadcast_to(share[:, None, :], (experts_all, 8, tokens_here))
        mixed = moe_ring(
            normed,
            hidden,
            share,
            expert_gate,
            expert_up,
            expert_down,
            experts_all,
            -(-capacity // 16) * 16,
        )
        return (hidden.astype(jnp.bfloat16), mixed)
    flat_routes = routes.reshape(-1)
    hits = (flat_routes[:, None] == jnp.arange(experts_all, dtype=jnp.int32)[None, :]).astype(
        jnp.int32
    )
    slot = jnp.sum(hits * (jnp.cumsum(hits, axis=0) - 1), axis=-1)
    target = flat_routes * capacity + slot
    source = jnp.arange(tokens_here * TOP, dtype=jnp.int32) // TOP
    outgoing = jnp.zeros((experts_all * capacity, D), jnp.bfloat16).at[target].set(normed[source])
    outgoing = outgoing.reshape(experts_all, capacity, D)
    arrived = lax.all_to_all(outgoing, "ctx", split_axis=0, concat_axis=0, tiled=True)
    senders = arrived.shape[0] // EXP_DEV
    width = arrived.shape[1]
    inputs = (
        arrived.reshape(senders, EXP_DEV, width, D)
        .transpose(1, 0, 2, 3)
        .reshape(EXP_DEV, senders * width, D)
    )
    gate = jnp.einsum("erd,edf->erf", inputs, expert_gate, preferred_element_type=jnp.float32)
    upper = jnp.einsum("erd,edf->erf", inputs, expert_up, preferred_element_type=jnp.float32)
    act = (jax.nn.silu(gate) * upper).astype(jnp.bfloat16)
    result = jnp.einsum(
        "erf,efd->erd", act, expert_down, preferred_element_type=jnp.float32
    ).astype(jnp.bfloat16)
    result = (
        result.reshape(EXP_DEV, senders, width, D)
        .transpose(1, 0, 2, 3)
        .reshape(senders * EXP_DEV, width, D)
    )
    returned = lax.all_to_all(result, "ctx", split_axis=0, concat_axis=0, tiled=True)
    returned = returned.reshape(experts_all * capacity, D)
    picked = jnp.take(returned, target, axis=0).reshape(tokens_here, TOP, D)
    blended = jnp.sum(combine[:, :, None] * picked.astype(jnp.float32), axis=1)
    return (hidden.astype(jnp.bfloat16), (hidden + blended).astype(jnp.bfloat16))


def solution(mesh):
    in_specs = (
        P(("groups", "ctx"), None),
        P(("groups", "ctx"), None),
        P(("groups", "ctx"), None),
        P(("groups", "ctx")),
        P("ctx", None),
        P(),
        P(),
        P(("groups", "ctx"), None),
        P(("groups", "ctx"), None),
        P("ctx", None, None),
        P("ctx", None, None),
        P("ctx", None, None),
    )
    out_specs = (P(("groups", "ctx"), None), P(("groups", "ctx"), None))
    return jax.shard_map(body, mesh=mesh, in_specs=in_specs, out_specs=out_specs, check_vma=False)
```

```python
import functools
import math

import jax
import jax.numpy as jnp
from jax import lax
from jax.experimental import pallas as pl
from jax.experimental.pallas import tpu as pltpu
from jax.sharding import PartitionSpec as P

D = 2048
HQ = 16
KVH = 4
HD = 128
TOP = 8
EXP_DEV = 1
NB = 4


def normalize(x):
    return x * lax.rsqrt(jnp.mean(x * x, axis=-1, keepdims=True) + 1e-06)


RING_BYTES = 16 * 2**20


def chip_at(position, chips):
    depth = chips // 2
    y = position // depth
    return (position * (1 - y) + (chips - 1 - position) * y) * 2 + y


def layer_kernel(
    n,
    cap,
    queries,
    keys,
    values,
    blocks,
    weight_own,
    key_gain,
    norm_gain,
    share,
    gate_hbm,
    up_hbm,
    down_hbm,
    projected,
    out,
    normed,
    hidden,
    att,
    wg,
    sums_own,
    sums,
    gate_w,
    up_w,
    down_w,
    tok,
    wbuf,
    rows_in,
    act,
    place,
    comb,
    mine,
    outgo,
    theirs,
    ring_in,
    load_sem,
    s_send,
    s_recv,
    wg_send,
    wg_recv,
    wx_send,
    wx_recv,
    wp_send,
    wp_recv,
    w_send,
    w_recv,
    ag_send,
    ag_recv,
    pt_send,
    pt_recv,
    y_send,
    y_recv,
    rs_send_sem,
    rs_recv_sem,
):
    tokens = normed.shape[0]
    half = tokens // 2
    width = normed.shape[1]
    ff = gate_w.shape[1]
    chips = n // 2
    far = chips // 2
    me = lax.axis_index("ctx")
    core = me % 2
    y = (me // 2) % 2
    z = me // 4
    pos = z * (1 - y) + (chips - 1 - z) * y
    partner = me + 1 - 2 * core
    ahead = chip_at((pos + 1) % chips, chips) * 2 + core
    behind = chip_at((pos + chips - 1) % chips, chips) * 2 + core
    neighbour = (ahead, behind)

    loads = [
        pltpu.make_async_copy(a, b, load_sem.at[k])
        for k, (a, b) in enumerate(((gate_hbm, gate_w), (up_hbm, up_w), (down_hbm, down_w)))
    ]
    for load in loads:
        load.start()

    barrier = pltpu.get_barrier_semaphore()
    across = 1 - lax.axis_index("groups")

    def greet(k, _):
        pl.semaphore_signal(barrier, inc=1, device_id={"ctx": (me + k) % n})
        return 0

    lax.fori_loop(1, n, greet, 0)
    pl.semaphore_signal(barrier, inc=1, device_id={"groups": across})

    def mean_of(ref):
        ids = blocks[...]
        member = jnp.where(
            ids == lax.broadcasted_iota(jnp.int32, ids.shape, 0) % NB, 1.0, 0.0
        )
        count = jnp.sum(member, axis=1, keepdims=True)
        return (
            jnp.dot(member.astype(jnp.bfloat16), ref[...], preferred_element_type=jnp.float32)
            / count
        )

    kmean, vmean = mean_of(keys), mean_of(values)
    upper = lax.broadcasted_iota(jnp.int32, (2 * NB, HD), 0) < NB
    for g in range(KVH):
        cols = slice(g * HD, (g + 1) * HD)
        sums_own[:, cols] = jnp.where(
            upper, normalize(kmean[:, cols]) * key_gain[...], normalize(vmean[:, cols])
        ).astype(jnp.bfloat16)
    pl.semaphore_wait(barrier, n)

    def s_copy(k):
        target = (me + k) % n
        return pltpu.make_async_remote_copy(
            src_ref=sums_own,
            dst_ref=sums.at[me],
            send_sem=s_send.at[k],
            recv_sem=s_recv.at[k],
            device_id={"ctx": target},
        )

    def s_start(k, _):
        s_copy(k).start()
        return 0

    def s_wait(k, _):
        s_copy(k).wait()
        return 0

    lax.fori_loop(1, n, s_start, 0)
    sums[me] = sums_own[...]

    def rows(h):
        return pl.ds(h * half, half)

    def chip(offset):
        return (pos + offset + chips) % chips

    def ag_copy(d, step, h):
        sign = 1 - 2 * d
        q = chip(-sign * (step - 1))
        src = normed.at[rows(h)] if step == 1 else tok.at[q, core, rows(h)]
        return pltpu.make_async_remote_copy(
            src_ref=src,
            dst_ref=tok.at[q, core, rows(h)],
            send_sem=ag_send.at[d, step - 1, h],
            recv_sem=ag_recv.at[d, step - 1, h],
            device_id={"ctx": neighbour[d]},
        )

    def pt_copy(offset, h):
        q = chip(offset)
        src = normed.at[rows(h)] if offset == 0 else tok.at[q, core, rows(h)]
        return pltpu.make_async_remote_copy(
            src_ref=src,
            dst_ref=tok.at[q, core, rows(h)],
            send_sem=pt_send.at[offset % chips, h],
            recv_sem=pt_recv.at[offset % chips, h],
            device_id={"ctx": partner},
        )

    def order(d):
        return (0, 1) if d == 0 else (1, 0)

    wrows = weight_own.shape[0]
    side = 3 * wrows // 8
    middle = wrows - 2 * side
    group = 1 - across
    mine_side = group * (side + middle)
    other_side = across * (side + middle)

    def w_rows(kind):
        if kind == 0:
            return mine_side, side
        if kind == 1:
            return side, middle
        return other_side, side

    def w_at(q, kind):
        start, size = w_rows(kind)
        return wg.at[q, pl.ds(core * wrows + start, size)]

    def w_first(kind):
        start, size = w_rows(kind)
        return weight_own.at[pl.ds(start, size)]

    def wg_copy(d, step, h):
        sign = 1 - 2 * d
        q = chip(-sign * (step - 1))
        return pltpu.make_async_remote_copy(
            src_ref=w_first(h) if step == 1 else w_at(q, h),
            dst_ref=w_at(q, h),
            send_sem=wg_send.at[d, step - 1, h],
            recv_sem=wg_recv.at[d, step - 1, h],
            device_id={"ctx": neighbour[d]},
        )

    def wx_copy(offset):
        q = chip(offset)
        return pltpu.make_async_remote_copy(
            src_ref=w_at(q, 0),
            dst_ref=w_at(q, 0),
            send_sem=wx_send.at[offset % chips],
            recv_sem=wx_recv.at[offset % chips],
            device_id={"groups": across},
        )

    def wp_copy(offset, kind):
        q = chip(offset)
        return pltpu.make_async_remote_copy(
            src_ref=w_first(kind) if offset == 0 else w_at(q, kind),
            dst_ref=w_at(q, kind),
            send_sem=wp_send.at[offset % chips, kind],
            recv_sem=wp_recv.at[offset % chips, kind],
            device_id={"ctx": partner},
        )

    for k in range(2):
        for d in range(2):
            wg_copy(d, 1, order(d)[k]).start()
    for kind in range(3):
        wp_copy(0, kind).start()
    wg[pos, pl.ds(pl.multiple_of(core * wrows, wrows), wrows)] = weight_own[...]

    def w_copy(k):
        target = (me + k) % n
        return pltpu.make_async_remote_copy(
            src_ref=share.at[target],
            dst_ref=wbuf.at[pos * 2 + core],
            send_sem=w_send.at[k],
            recv_sem=w_recv.at[k],
            device_id={"ctx": target},
        )

    def w_start(k, _):
        w_copy(k).start()
        return 0

    def w_wait(k, _):
        w_copy(k).wait()
        return 0

    lax.fori_loop(1, n, w_start, 0)
    wbuf[pos * 2 + core] = share[me]
    lax.fori_loop(1, n, s_wait, 0)

    many = HQ // KVH
    scale = 1.0 / math.sqrt(HD)
    tall = (many * tokens, tokens)
    causal = lax.broadcasted_iota(jnp.int32, tall, 0) % tokens >= lax.broadcasted_iota(
        jnp.int32, tall, 1
    )
    far_shape = (many * tokens, n * 2 * NB)
    entry = lax.broadcasted_iota(jnp.int32, far_shape, 1)
    seen = (entry % (2 * NB) < NB) & (entry // (2 * NB) < me)
    contract_last = (((1,), (1,)), ((), ()))

    def attend(g):
        cols = slice(g * HD, (g + 1) * HD)
        heads = [slice((g * many + i) * HD, (g * many + i + 1) * HD) for i in range(many)]
        q = jnp.concatenate([queries[:, c] for c in heads], axis=0)
        table = sums[:, :, cols].astype(jnp.float32).reshape(n * 2 * NB, HD)
        shifted = jnp.concatenate([table[NB:], table[:NB]], axis=0).astype(jnp.bfloat16)
        table = table.astype(jnp.bfloat16)
        near = (
            lax.dot_general(q, keys[:, cols], contract_last, preferred_element_type=jnp.float32)
            * scale
        )
        near = jnp.where(causal, near, -jnp.inf)
        remote = lax.dot_general(q, table, contract_last, preferred_element_type=jnp.float32) * scale
        remote = jnp.where(seen, remote, -jnp.inf)
        top = jnp.maximum(
            jnp.max(near, axis=1, keepdims=True), jnp.max(remote, axis=1, keepdims=True)
        )
        near, remote = jnp.exp(near - top), jnp.exp(remote - top)
        total = jnp.sum(near, axis=1, keepdims=True) + jnp.sum(remote, axis=1, keepdims=True)
        near, remote = (near / total).astype(jnp.bfloat16), (remote / total).astype(jnp.bfloat16)
        result = jnp.dot(
            near, values[:, cols], preferred_element_type=jnp.float32
        ) + jnp.dot(remote, shifted, preferred_element_type=jnp.float32)
        result = result.astype(jnp.bfloat16)
        for i, c in enumerate(heads):
            att[:, c] = result[i * tokens : (i + 1) * tokens]

    def project(offset):
        q = chip(offset)
        for kind in range(3):
            wp_copy(offset, kind).wait_recv()
        place_at = pl.multiple_of(chip_at(q, chips) * 2 * wrows, 2 * wrows)
        left = att[:, pl.ds(place_at, 2 * wrows)]

        def tile(k, _):
            cols = pl.ds(pl.multiple_of(k * 512, 512), 512)
            part = jnp.dot(left, wg[q, :, cols], preferred_element_type=jnp.float32)
            hidden[:, cols] = part if offset == 0 else hidden[:, cols] + part
            return 0

        lax.fori_loop(0, width // 512, tile, 0)

    def w_step(step, k):
        for d in range(2):
            h = order(d)[k]
            sign = 1 - 2 * d
            wg_copy(d, step, h).wait_recv()
            if step + 1 < far or (step + 1 == far and k == 0):
                wg_copy(d, step + 1, h).start()
            if h == 0:
                wx_copy(-sign * step).start()
            wp_copy(-sign * step, h).start()

    def x_step(offset):
        wx_copy(offset).wait_recv()
        wp_copy(offset, 2).start()

    attend(0)
    attend(1)
    w_step(1, 0)
    attend(2)
    w_step(1, 1)
    attend(3)
    for step in range(2, far):
        w_step(step, 0)
        x_step(1 - step)
        x_step(step - 1)
        if step == 2:
            project(0)
        else:
            project(2 - step)
        w_step(step, 1)
        if step > 2:
            project(step - 2)
    w_step(far, 0)
    x_step(1 - far)
    x_step(far - 1)
    project(2 - far)
    project(far - 2)
    x_step(far)
    project(1 - far)
    project(far - 1)
    project(far)
    for h in range(2):
        hid = hidden[rows(h)]
        projected[rows(h)] = hid.astype(jnp.bfloat16)
        tidy = (normalize(hid) * norm_gain[...]).astype(jnp.bfloat16)
        normed[rows(h)] = tidy
        tok[pos, core, rows(h)] = tidy

    for k in range(2):
        for d in range(2):
            ag_copy(d, 1, order(d)[k]).start()
    for h in range(2):
        pt_copy(0, h).start()

    lax.fori_loop(1, n, w_wait, 0)
    for load in loads:
        load.wait()

    def y_copy(offset):
        q = chip(offset)
        return pltpu.make_async_remote_copy(
            src_ref=outgo.at[q],
            dst_ref=theirs.at[q],
            send_sem=y_send.at[offset % chips],
            recv_sem=y_recv.at[offset % chips],
            device_id={"ctx": partner},
        )

    def compute(offset):
        q = chip(offset)
        for h in range(2):
            pt_copy(offset, h).wait_recv()
        earlier = lax.broadcasted_iota(jnp.int32, (tokens, tokens), 0) < lax.broadcasted_iota(
            jnp.int32, (tokens, tokens), 1
        )
        earlier = jnp.where(earlier, 1.0, 0.0).astype(jnp.bfloat16)
        line = lax.broadcasted_iota(jnp.int32, (cap, tokens), 0).astype(jnp.float32)
        for rel in range(2):
            side = (core + rel) % 2
            weight = wbuf[q * 2 + side]
            chosen = jnp.where(weight > 0.0, 1.0, 0.0)
            slot = jnp.dot(chosen.astype(jnp.bfloat16), earlier, preferred_element_type=jnp.float32)
            slot = jnp.where(weight > 0.0, slot, -1.0)
            hit = jnp.broadcast_to(slot[0:1], (cap, tokens)) == line
            pick = jnp.where(hit, 1.0, 0.0).astype(jnp.bfloat16)
            place[rel] = pick
            scaled = jnp.where(hit, jnp.broadcast_to(weight[0:1], (cap, tokens)), 0.0)
            comb[rel] = jnp.broadcast_to(jnp.sum(scaled, axis=1, keepdims=True), (cap, 128))
            for c in range(0, width, 512):
                rows_in[rel * cap : (rel + 1) * cap, c : c + 512] = jnp.dot(
                    pick, tok[q, side, :, c : c + 512], preferred_element_type=jnp.float32
                ).astype(jnp.bfloat16)

        def in_tile(k, _):
            cols = pl.ds(pl.multiple_of(k * 256, 256), 256)
            x = rows_in[...]
            g = jnp.dot(x, gate_w[:, cols], preferred_element_type=jnp.float32)
            u = jnp.dot(x, up_w[:, cols], preferred_element_type=jnp.float32)
            act[:, cols] = (g / (1.0 + jnp.exp(-g)) * u).astype(jnp.bfloat16)
            return 0

        lax.fori_loop(0, ff // 256, in_tile, 0)

        def out_tile(k, _):
            cols = pl.ds(pl.multiple_of(k * 512, 512), 512)
            r = jnp.dot(act[...], down_w[:, cols], preferred_element_type=jnp.float32)
            r = r.astype(jnp.bfloat16).astype(jnp.float32)
            for rel, dest in ((0, mine), (1, outgo)):
                part = r[rel * cap : (rel + 1) * cap] * comb[rel][:, 0:1]
                dest[q, :, cols] = lax.dot_general(
                    place[rel],
                    part.astype(jnp.bfloat16),
                    (((0,), (0,)), ((), ())),
                    preferred_element_type=jnp.float32,
                ).astype(jnp.bfloat16)
            return 0

        lax.fori_loop(0, width // 512, out_tile, 0)
        y_copy(offset).start()

    for step in range(1, far):
        for k in range(2):
            for d in range(2):
                h = order(d)[k]
                sign = 1 - 2 * d
                ag_copy(d, step, h).wait_recv()
                if step + 1 < far or k == 0:
                    ag_copy(d, step + 1, h).start()
                pt_copy(-sign * step, h).start()
            if step == 1:
                if k == 0:
                    compute(0)
            else:
                compute((step - 1) * (2 * k - 1))
    compute(1 - far)
    compute(far - 1)
    for d in range(2):
        h = order(d)[0]
        ag_copy(d, far, h).wait_recv()
        pt_copy(far, h).start()

    def sum_of(q, h):
        return mine[q, rows(h)].astype(jnp.float32) + theirs[q, rows(h)].astype(jnp.float32)

    def rs_copy(d, step, h, src):
        return pltpu.make_async_remote_copy(
            src_ref=src,
            dst_ref=ring_in.at[d, step - 1, h],
            send_sem=rs_send_sem.at[d, step - 1, h],
            recv_sem=rs_recv_sem.at[d, step - 1, h],
            device_id={"ctx": neighbour[d]},
        )

    def rs_step(d, step, k):
        h = order(d)[k]
        sign = 1 - 2 * d
        q = chip(sign * (far + 1 - step))
        if step == 1 or (step == 2 and k == 1):
            mine[q, rows(h)] = sum_of(q, h).astype(jnp.bfloat16)
            src = mine.at[q, rows(h)]
        else:
            src = ring_in.at[d, step - 2, h]
            rs_copy(d, step - 1, h, src).wait_recv()
            ring_in[d, step - 2, h] = (
                ring_in[d, step - 2, h].astype(jnp.float32) + sum_of(q, h)
            ).astype(jnp.bfloat16)
        rs_copy(d, step, h, src).start()

    for offset in range(chips):
        if offset != far:
            y_copy(offset).wait_recv()
    for d in range(2):
        rs_step(d, 2, 1)
    compute(far)
    y_copy(far).wait_recv()
    sends = [(1, 0)]
    for step in range(2, far + 1):
        if step < far:
            sends += [(step + 1, 1)]
        sends += [(step, 0)]
    for step, k in sends:
        for d in range(2):
            rs_step(d, step, k)
    for h in range(2):
        total = hidden[rows(h)] + sum_of(pos, h)
        for d in range(2):
            rs_copy(d, far, h, ring_in.at[d, far - 1, h]).wait_recv()
            total = total + ring_in[d, far - 1, h].astype(jnp.float32)
        out[rows(h)] = total.astype(jnp.bfloat16)

    for d in range(2):
        for step in range(1, far + 1):
            for k in range(2):
                h = order(d)[k]
                if step < far or k == 0:
                    ag_copy(d, step, h).wait_send()
                if step > 1 or k == 0:
                    rs_copy(d, step, h, ring_in.at[d, step - 1, h]).wait_send()
    for offset in range(chips):
        for h in range(2):
            pt_copy(offset, h).wait_send()
        y_copy(offset).wait_send()


    for d in range(2):
        for step in range(1, far + 1):
            for k in range(2):
                if step < far or k == 0:
                    wg_copy(d, step, order(d)[k]).wait_send()
    for offset in range(chips):
        if offset > 0:
            wx_copy(offset).wait_send()
        for kind in range(3):
            wp_copy(offset, kind).wait_send()


def layer_ring(
    queries,
    keys,
    values,
    block_ids,
    out_weight,
    summary_gain,
    norm_gain,
    share,
    expert_gate,
    expert_up,
    expert_down,
    n,
    cap,
):
    tokens, width = queries.shape
    ff = expert_gate.shape[-1]
    chips = n // 2
    far = chips // 2
    vmem = pl.BlockSpec(memory_space=pltpu.VMEM)
    hbm = pl.BlockSpec(memory_space=pl.ANY)
    dma = pltpu.SemaphoreType.DMA
    bf16, f32 = jnp.bfloat16, jnp.float32
    result = jax.ShapeDtypeStruct((tokens, width), bf16)
    return pl.pallas_call(
        functools.partial(layer_kernel, n, cap),
        out_shape=(result, result),
        in_specs=[vmem] * 8 + [hbm] * 3,
        out_specs=(vmem, vmem),
        scratch_shapes=[
            pltpu.VMEM((tokens, width), bf16),
            pltpu.VMEM((tokens, width), f32),
            pltpu.VMEM((tokens, width), bf16),
            pltpu.VMEM((chips, 2 * out_weight.shape[0], width), bf16),
            pltpu.VMEM((2 * NB, KVH * HD), bf16),
            pltpu.VMEM((n, 2 * NB, KVH * HD), bf16),
            pltpu.VMEM((width, ff), bf16),
            pltpu.VMEM((width, ff), bf16),
            pltpu.VMEM((ff, width), bf16),
            pltpu.VMEM((chips, 2, tokens, width), bf16),
            pltpu.VMEM((n, 8, tokens), f32),
            pltpu.VMEM((2 * cap, width), bf16),
            pltpu.VMEM((2 * cap, ff), bf16),
            pltpu.VMEM((2, cap, tokens), bf16),
            pltpu.VMEM((2, cap, 128), f32),
            pltpu.VMEM((chips, tokens, width), bf16),
            pltpu.VMEM((chips, tokens, width), bf16),
            pltpu.VMEM((chips, tokens, width), bf16),
            pltpu.VMEM((2, far, 2, tokens // 2, width), bf16),
            dma((3,)),
            dma((n,)),
            dma((n,)),
            dma((2, far, 2)),
            dma((2, far, 2)),
            dma((chips,)),
            dma((chips,)),
            dma((chips, 3)),
            dma((chips, 3)),
            dma((n,)),
            dma((n,)),
            dma((2, far, 2)),
            dma((2, far, 2)),
            dma((chips, 2)),
            dma((chips, 2)),
            dma((chips,)),
            dma((chips,)),
            dma((2, far, 2)),
            dma((2, far, 2)),
        ],
        compiler_params=pltpu.CompilerParams(
            collective_id=1, has_side_effects=True, vmem_limit_bytes=62 * 2**20
        ),
    )(
        queries,
        keys,
        values,
        jnp.broadcast_to(block_ids[None, :], (2 * NB, tokens)),
        out_weight,
        summary_gain[None, :],
        norm_gain[None, :],
        share,
        expert_gate[0],
        expert_up[0],
        expert_down[0],
    )


def body(
    queries,
    keys,
    values,
    block_ids,
    out_weight,
    summary_gain,
    norm_gain,
    routes,
    route_scores,
    expert_gate,
    expert_up,
    expert_down,
):
    tokens_here = queries.shape[0]
    combine = route_scores / jnp.sum(route_scores, axis=-1, keepdims=True)
    experts_all = EXP_DEV * lax.axis_size("ctx")
    capacity = max(2, 5 * tokens_here * TOP // (4 * experts_all))
    chips = experts_all // 2
    fits = experts_all * tokens_here * D * 2 <= RING_BYTES
    if fits and chips % 4 == 0 and lax.axis_size("groups") == 2:
        named = routes[:, :, None] == jnp.arange(experts_all, dtype=jnp.int32)[None, None, :]
        share = jnp.sum(jnp.where(named, combine[:, :, None], 0.0), axis=1).T
        share = jnp.broadcast_to(share[:, None, :], (experts_all, 8, tokens_here))
        return layer_ring(
            queries,
            keys,
            values,
            block_ids,
            out_weight,
            summary_gain,
            norm_gain,
            share,
            expert_gate,
            expert_up,
            expert_down,
            experts_all,
            -(-capacity // 16) * 16,
        )
    group = HQ // KVH
    scale = 1.0 / math.sqrt(HD)
    member = block_ids[None, :] == jnp.arange(NB, dtype=jnp.int32)[:, None]
    count = jnp.sum(member.astype(jnp.float32), axis=-1)
    indicator = member.astype(jnp.bfloat16)
    kmean = jnp.dot(indicator, keys, preferred_element_type=jnp.float32) / count[:, None]
    vmean = jnp.dot(indicator, values, preferred_element_type=jnp.float32) / count[:, None]
    summary_keys = (
        (normalize(kmean.reshape(NB, KVH, HD)) * summary_gain)
        .astype(jnp.bfloat16)
        .reshape(NB, KVH * HD)
    )
    summary_values = (
        normalize(vmean.reshape(NB, KVH, HD)).astype(jnp.bfloat16).reshape(NB, KVH * HD)
    )
    summaries = lax.all_gather(
        jnp.concatenate([summary_keys, summary_values], axis=1), "ctx", axis=0, tiled=True
    )
    all_keys, all_values = summaries[:, : KVH * HD], summaries[:, KVH * HD :]
    index = lax.axis_index("ctx")
    query = queries.reshape(tokens_here, KVH, group, HD)
    key_loc = keys.reshape(tokens_here, KVH, HD)
    remote_keys = all_keys.reshape(-1, KVH, HD)
    causal = jnp.arange(tokens_here)[:, None] >= jnp.arange(tokens_here)[None, :]
    owner = jnp.arange(remote_keys.shape[0], dtype=jnp.int32) // NB
    local = jnp.einsum("tkgd,skd->kgts", query, key_loc, preferred_element_type=jnp.float32) * scale
    local = jnp.where(causal[None, None], local, -jnp.inf)
    remote = (
        jnp.einsum("tkgd,skd->kgts", query, remote_keys, preferred_element_type=jnp.float32) * scale
    )
    remote = jnp.where((owner < index)[None, None, None, :], remote, -jnp.inf)
    scores = jnp.concatenate([local, remote], axis=-1)
    top = jnp.max(scores, axis=-1, keepdims=True)
    expo = jnp.exp(scores - top)
    weights = (expo / jnp.sum(expo, axis=-1, keepdims=True)).astype(jnp.bfloat16)
    every_value = jnp.concatenate(
        [values.reshape(tokens_here, KVH, HD), all_values.reshape(-1, KVH, HD)], axis=0
    )
    attended = jnp.einsum(
        "kgts,skd->tkgd", weights, every_value, preferred_element_type=jnp.float32
    )
    attended = attended.reshape(tokens_here, HQ * HD).astype(jnp.bfloat16)
    hidden = jnp.dot(
        attended,
        lax.all_gather(out_weight, "ctx", axis=0, tiled=True),
        preferred_element_type=jnp.float32,
    )
    normed = (normalize(hidden) * norm_gain).astype(jnp.bfloat16)
    flat_routes = routes.reshape(-1)
    hits = (flat_routes[:, None] == jnp.arange(experts_all, dtype=jnp.int32)[None, :]).astype(
        jnp.int32
    )
    slot = jnp.sum(hits * (jnp.cumsum(hits, axis=0) - 1), axis=-1)
    target = flat_routes * capacity + slot
    source = jnp.arange(tokens_here * TOP, dtype=jnp.int32) // TOP
    outgoing = jnp.zeros((experts_all * capacity, D), jnp.bfloat16).at[target].set(normed[source])
    outgoing = outgoing.reshape(experts_all, capacity, D)
    arrived = lax.all_to_all(outgoing, "ctx", split_axis=0, concat_axis=0, tiled=True)
    senders = arrived.shape[0] // EXP_DEV
    width = arrived.shape[1]
    inputs = (
        arrived.reshape(senders, EXP_DEV, width, D)
        .transpose(1, 0, 2, 3)
        .reshape(EXP_DEV, senders * width, D)
    )
    gate = jnp.einsum("erd,edf->erf", inputs, expert_gate, preferred_element_type=jnp.float32)
    upper = jnp.einsum("erd,edf->erf", inputs, expert_up, preferred_element_type=jnp.float32)
    act = (jax.nn.silu(gate) * upper).astype(jnp.bfloat16)
    result = jnp.einsum(
        "erf,efd->erd", act, expert_down, preferred_element_type=jnp.float32
    ).astype(jnp.bfloat16)
    result = (
        result.reshape(EXP_DEV, senders, width, D)
        .transpose(1, 0, 2, 3)
        .reshape(senders * EXP_DEV, width, D)
    )
    returned = lax.all_to_all(result, "ctx", split_axis=0, concat_axis=0, tiled=True)
    returned = returned.reshape(experts_all * capacity, D)
    picked = jnp.take(returned, target, axis=0).reshape(tokens_here, TOP, D)
    blended = jnp.sum(combine[:, :, None] * picked.astype(jnp.float32), axis=1)
    return (hidden.astype(jnp.bfloat16), (hidden + blended).astype(jnp.bfloat16))


def solution(mesh):
    in_specs = (
        P(("groups", "ctx"), None),
        P(("groups", "ctx"), None),
        P(("groups", "ctx"), None),
        P(("groups", "ctx")),
        P("ctx", None),
        P(),
        P(),
        P(("groups", "ctx"), None),
        P(("groups", "ctx"), None),
        P("ctx", None, None),
        P("ctx", None, None),
        P("ctx", None, None),
    )
    out_specs = (P(("groups", "ctx"), None), P(("groups", "ctx"), None))
    return jax.shard_map(body, mesh=mesh, in_specs=in_specs, out_specs=out_specs, check_vma=False)
```

```python
import functools
import math

import jax
import jax.numpy as jnp
from jax import lax
from jax.experimental import pallas as pl
from jax.experimental.pallas import tpu as pltpu
from jax.sharding import PartitionSpec as P

D = 2048
HQ = 16
KVH = 4
HD = 128
TOP = 8
EXP_DEV = 1
NB = 4


def normalize(x):
    return x * lax.rsqrt(jnp.mean(x * x, axis=-1, keepdims=True) + 1e-06)


RING_BYTES = 16 * 2**20


def chip_at(position, chips):
    depth = chips // 2
    y = position // depth
    return (position * (1 - y) + (chips - 1 - position) * y) * 2 + y


def layer_kernel(
    n,
    cap,
    queries,
    keys,
    values,
    blocks,
    weight_own,
    key_gain,
    norm_gain,
    routes,
    route_scores,
    gate_hbm,
    up_hbm,
    down_hbm,
    projected,
    out,
    normed,
    hidden,
    att,
    wg,
    sums_own,
    sums,
    share,
    gate_w,
    up_w,
    down_w,
    tok,
    wbuf,
    rows_in,
    act,
    place,
    comb,
    mine,
    outgo,
    theirs,
    ring_in,
    load_sem,
    s_send,
    s_recv,
    wg_send,
    wg_recv,
    wx_send,
    wx_recv,
    wp_send,
    wp_recv,
    w_send,
    w_recv,
    ag_send,
    ag_recv,
    pt_send,
    pt_recv,
    y_send,
    y_recv,
    rs_send_sem,
    rs_recv_sem,
):
    tokens = normed.shape[0]
    half = tokens // 2
    width = normed.shape[1]
    ff = gate_w.shape[1]
    chips = n // 2
    far = chips // 2
    me = lax.axis_index("ctx")
    core = me % 2
    y = (me // 2) % 2
    z = me // 4
    pos = z * (1 - y) + (chips - 1 - z) * y
    partner = me + 1 - 2 * core
    ahead = chip_at((pos + 1) % chips, chips) * 2 + core
    behind = chip_at((pos + chips - 1) % chips, chips) * 2 + core
    neighbour = (ahead, behind)

    loads = [
        pltpu.make_async_copy(a, b, load_sem.at[k])
        for k, (a, b) in enumerate(((gate_hbm, gate_w), (up_hbm, up_w), (down_hbm, down_w)))
    ]
    for load in loads:
        load.start()

    barrier = pltpu.get_barrier_semaphore()
    across = 1 - lax.axis_index("groups")

    def greet(k, _):
        pl.semaphore_signal(barrier, inc=1, device_id={"ctx": (me + k) % n})
        return 0

    lax.fori_loop(1, n, greet, 0)
    pl.semaphore_signal(barrier, inc=1, device_id={"groups": across})

    def mean_of(ref):
        shape = (2 * NB, tokens)
        ids = jnp.broadcast_to(blocks[...], shape)
        member = jnp.where(ids == lax.broadcasted_iota(jnp.int32, shape, 0) % NB, 1.0, 0.0)
        count = jnp.sum(member, axis=1, keepdims=True)
        return (
            jnp.dot(member.astype(jnp.bfloat16), ref[...], preferred_element_type=jnp.float32)
            / count
        )

    kmean, vmean = mean_of(keys), mean_of(values)
    upper = lax.broadcasted_iota(jnp.int32, (2 * NB, HD), 0) < NB
    for g in range(KVH):
        cols = slice(g * HD, (g + 1) * HD)
        sums_own[:, cols] = jnp.where(
            upper, normalize(kmean[:, cols]) * key_gain[...], normalize(vmean[:, cols])
        ).astype(jnp.bfloat16)
    pl.semaphore_wait(barrier, n)

    def s_copy(k):
        target = (me + k) % n
        return pltpu.make_async_remote_copy(
            src_ref=sums_own,
            dst_ref=sums.at[me],
            send_sem=s_send.at[k],
            recv_sem=s_recv.at[k],
            device_id={"ctx": target},
        )

    def s_start(k, _):
        s_copy(k).start()
        return 0

    def s_wait(k, _):
        s_copy(k).wait()
        return 0

    lax.fori_loop(1, n, s_start, 0)
    sums[me] = sums_own[...]

    def rows(h):
        return pl.ds(h * half, half)

    def chip(offset):
        return (pos + offset + chips) % chips

    def ag_copy(d, step, h):
        sign = 1 - 2 * d
        q = chip(-sign * (step - 1))
        src = normed.at[rows(h)] if step == 1 else tok.at[q, core, rows(h)]
        return pltpu.make_async_remote_copy(
            src_ref=src,
            dst_ref=tok.at[q, core, rows(h)],
            send_sem=ag_send.at[d, step - 1, h],
            recv_sem=ag_recv.at[d, step - 1, h],
            device_id={"ctx": neighbour[d]},
        )

    def pt_copy(offset, h):
        q = chip(offset)
        src = normed.at[rows(h)] if offset == 0 else tok.at[q, core, rows(h)]
        return pltpu.make_async_remote_copy(
            src_ref=src,
            dst_ref=tok.at[q, core, rows(h)],
            send_sem=pt_send.at[offset % chips, h],
            recv_sem=pt_recv.at[offset % chips, h],
            device_id={"ctx": partner},
        )

    def order(d):
        return (0, 1) if d == 0 else (1, 0)

    wrows = weight_own.shape[0]
    side = 3 * wrows // 8
    middle = wrows - 2 * side
    group = 1 - across
    mine_side = group * (side + middle)
    other_side = across * (side + middle)

    def w_rows(kind):
        if kind == 0:
            return mine_side, side
        if kind == 1:
            return side, middle
        return other_side, side

    def w_at(q, kind):
        start, size = w_rows(kind)
        return wg.at[q, pl.ds(core * wrows + start, size)]

    def w_first(kind):
        start, size = w_rows(kind)
        return weight_own.at[pl.ds(start, size)]

    def wg_copy(d, step, h):
        sign = 1 - 2 * d
        q = chip(-sign * (step - 1))
        return pltpu.make_async_remote_copy(
            src_ref=w_first(h) if step == 1 else w_at(q, h),
            dst_ref=w_at(q, h),
            send_sem=wg_send.at[d, step - 1, h],
            recv_sem=wg_recv.at[d, step - 1, h],
            device_id={"ctx": neighbour[d]},
        )

    def wx_copy(offset):
        q = chip(offset)
        return pltpu.make_async_remote_copy(
            src_ref=w_at(q, 0),
            dst_ref=w_at(q, 0),
            send_sem=wx_send.at[offset % chips],
            recv_sem=wx_recv.at[offset % chips],
            device_id={"groups": across},
        )

    def wp_copy(offset, kind):
        q = chip(offset)
        return pltpu.make_async_remote_copy(
            src_ref=w_first(kind) if offset == 0 else w_at(q, kind),
            dst_ref=w_at(q, kind),
            send_sem=wp_send.at[offset % chips, kind],
            recv_sem=wp_recv.at[offset % chips, kind],
            device_id={"ctx": partner},
        )

    for k in range(2):
        for d in range(2):
            wg_copy(d, 1, order(d)[k]).start()
    for kind in range(3):
        wp_copy(0, kind).start()
    wg[pos, pl.ds(pl.multiple_of(core * wrows, wrows), wrows)] = weight_own[...]

    def w_copy(k):
        target = (me + k) % n
        return pltpu.make_async_remote_copy(
            src_ref=share.at[target],
            dst_ref=wbuf.at[pos * 2 + core],
            send_sem=w_send.at[k],
            recv_sem=w_recv.at[k],
            device_id={"ctx": target},
        )

    def w_start(k, _):
        w_copy(k).start()
        return 0

    def w_wait(k, _):
        w_copy(k).wait()
        return 0

    chosen_scores = route_scores[...]
    combine = chosen_scores / jnp.sum(chosen_scores, axis=0, keepdims=True)
    expert = lax.broadcasted_iota(jnp.int32, (n, tokens), 0)
    table_of = jnp.zeros((n, tokens), jnp.float32)
    for c in range(TOP):
        table_of = table_of + jnp.where(routes[c : c + 1] == expert, combine[c : c + 1], 0.0)
    for e in range(n):
        share[e] = jnp.broadcast_to(table_of[e : e + 1], (8, tokens))
    lax.fori_loop(1, n, w_start, 0)
    wbuf[pos * 2 + core] = share[me]
    lax.fori_loop(1, n, s_wait, 0)

    many = HQ // KVH
    scale = 1.0 / math.sqrt(HD)
    tall = (many * tokens, tokens)
    causal = lax.broadcasted_iota(jnp.int32, tall, 0) % tokens >= lax.broadcasted_iota(
        jnp.int32, tall, 1
    )
    far_shape = (many * tokens, n * 2 * NB)
    entry = lax.broadcasted_iota(jnp.int32, far_shape, 1)
    seen = (entry % (2 * NB) < NB) & (entry // (2 * NB) < me)
    contract_last = (((1,), (1,)), ((), ()))

    def attend(g):
        cols = slice(g * HD, (g + 1) * HD)
        heads = [slice((g * many + i) * HD, (g * many + i + 1) * HD) for i in range(many)]
        q = jnp.concatenate([queries[:, c] for c in heads], axis=0)
        table = sums[:, :, cols].astype(jnp.float32).reshape(n * 2 * NB, HD)
        shifted = jnp.concatenate([table[NB:], table[:NB]], axis=0).astype(jnp.bfloat16)
        table = table.astype(jnp.bfloat16)
        near = (
            lax.dot_general(q, keys[:, cols], contract_last, preferred_element_type=jnp.float32)
            * scale
        )
        near = jnp.where(causal, near, -jnp.inf)
        remote = lax.dot_general(q, table, contract_last, preferred_element_type=jnp.float32) * scale
        remote = jnp.where(seen, remote, -jnp.inf)
        top = jnp.maximum(
            jnp.max(near, axis=1, keepdims=True), jnp.max(remote, axis=1, keepdims=True)
        )
        near, remote = jnp.exp(near - top), jnp.exp(remote - top)
        total = jnp.sum(near, axis=1, keepdims=True) + jnp.sum(remote, axis=1, keepdims=True)
        near, remote = (near / total).astype(jnp.bfloat16), (remote / total).astype(jnp.bfloat16)
        result = jnp.dot(
            near, values[:, cols], preferred_element_type=jnp.float32
        ) + jnp.dot(remote, shifted, preferred_element_type=jnp.float32)
        result = result.astype(jnp.bfloat16)
        for i, c in enumerate(heads):
            att[:, c] = result[i * tokens : (i + 1) * tokens]

    def project(offset):
        q = chip(offset)
        for kind in range(3):
            wp_copy(offset, kind).wait_recv()
        place_at = pl.multiple_of(chip_at(q, chips) * 2 * wrows, 2 * wrows)
        left = att[:, pl.ds(place_at, 2 * wrows)]

        def tile(k, _):
            cols = pl.ds(pl.multiple_of(k * 512, 512), 512)
            part = jnp.dot(left, wg[q, :, cols], preferred_element_type=jnp.float32)
            hidden[:, cols] = part if offset == 0 else hidden[:, cols] + part
            return 0

        lax.fori_loop(0, width // 512, tile, 0)

    def w_step(step, k):
        for d in range(2):
            h = order(d)[k]
            sign = 1 - 2 * d
            wg_copy(d, step, h).wait_recv()
            if step + 1 < far or (step + 1 == far and k == 0):
                wg_copy(d, step + 1, h).start()
            if h == 0:
                wx_copy(-sign * step).start()
            wp_copy(-sign * step, h).start()

    def x_step(offset):
        wx_copy(offset).wait_recv()
        wp_copy(offset, 2).start()

    attend(0)
    attend(1)
    w_step(1, 0)
    attend(2)
    w_step(1, 1)
    attend(3)
    for step in range(2, far):
        w_step(step, 0)
        x_step(1 - step)
        x_step(step - 1)
        if step == 2:
            project(0)
        else:
            project(2 - step)
        w_step(step, 1)
        if step > 2:
            project(step - 2)
    w_step(far, 0)
    x_step(1 - far)
    x_step(far - 1)
    project(2 - far)
    project(far - 2)
    x_step(far)
    project(1 - far)
    project(far - 1)
    project(far)
    for h in range(2):
        hid = hidden[rows(h)]
        projected[rows(h)] = hid.astype(jnp.bfloat16)
        tidy = (normalize(hid) * norm_gain[...]).astype(jnp.bfloat16)
        normed[rows(h)] = tidy
        tok[pos, core, rows(h)] = tidy

    for k in range(2):
        for d in range(2):
            ag_copy(d, 1, order(d)[k]).start()
    for h in range(2):
        pt_copy(0, h).start()

    lax.fori_loop(1, n, w_wait, 0)
    for load in loads:
        load.wait()

    def y_copy(offset):
        q = chip(offset)
        return pltpu.make_async_remote_copy(
            src_ref=outgo.at[q],
            dst_ref=theirs.at[q],
            send_sem=y_send.at[offset % chips],
            recv_sem=y_recv.at[offset % chips],
            device_id={"ctx": partner},
        )

    def compute(offset):
        q = chip(offset)
        for h in range(2):
            pt_copy(offset, h).wait_recv()
        earlier = lax.broadcasted_iota(jnp.int32, (tokens, tokens), 0) < lax.broadcasted_iota(
            jnp.int32, (tokens, tokens), 1
        )
        earlier = jnp.where(earlier, 1.0, 0.0).astype(jnp.bfloat16)
        line = lax.broadcasted_iota(jnp.int32, (cap, tokens), 0).astype(jnp.float32)
        for rel in range(2):
            side = (core + rel) % 2
            weight = wbuf[q * 2 + side]
            chosen = jnp.where(weight > 0.0, 1.0, 0.0)
            slot = jnp.dot(chosen.astype(jnp.bfloat16), earlier, preferred_element_type=jnp.float32)
            slot = jnp.where(weight > 0.0, slot, -1.0)
            hit = jnp.broadcast_to(slot[0:1], (cap, tokens)) == line
            pick = jnp.where(hit, 1.0, 0.0).astype(jnp.bfloat16)
            place[rel] = pick
            scaled = jnp.where(hit, jnp.broadcast_to(weight[0:1], (cap, tokens)), 0.0)
            comb[rel] = jnp.broadcast_to(jnp.sum(scaled, axis=1, keepdims=True), (cap, 128))
            for c in range(0, width, 512):
                rows_in[rel * cap : (rel + 1) * cap, c : c + 512] = jnp.dot(
                    pick, tok[q, side, :, c : c + 512], preferred_element_type=jnp.float32
                ).astype(jnp.bfloat16)

        def in_tile(k, _):
            cols = pl.ds(pl.multiple_of(k * 256, 256), 256)
            x = rows_in[...]
            g = jnp.dot(x, gate_w[:, cols], preferred_element_type=jnp.float32)
            u = jnp.dot(x, up_w[:, cols], preferred_element_type=jnp.float32)
            act[:, cols] = (g / (1.0 + jnp.exp(-g)) * u).astype(jnp.bfloat16)
            return 0

        lax.fori_loop(0, ff // 256, in_tile, 0)

        def out_tile(k, _):
            cols = pl.ds(pl.multiple_of(k * 512, 512), 512)
            r = jnp.dot(act[...], down_w[:, cols], preferred_element_type=jnp.float32)
            r = r.astype(jnp.bfloat16).astype(jnp.float32)
            for rel, dest in ((0, mine), (1, outgo)):
                part = r[rel * cap : (rel + 1) * cap] * comb[rel][:, 0:1]
                dest[q, :, cols] = lax.dot_general(
                    place[rel],
                    part.astype(jnp.bfloat16),
                    (((0,), (0,)), ((), ())),
                    preferred_element_type=jnp.float32,
                ).astype(jnp.bfloat16)
            return 0

        lax.fori_loop(0, width // 512, out_tile, 0)
        y_copy(offset).start()

    for step in range(1, far):
        for k in range(2):
            for d in range(2):
                h = order(d)[k]
                sign = 1 - 2 * d
                ag_copy(d, step, h).wait_recv()
                if step + 1 < far or k == 0:
                    ag_copy(d, step + 1, h).start()
                pt_copy(-sign * step, h).start()
            if step == 1:
                if k == 0:
                    compute(0)
            else:
                compute((step - 1) * (2 * k - 1))
    compute(1 - far)
    compute(far - 1)
    for d in range(2):
        h = order(d)[0]
        ag_copy(d, far, h).wait_recv()
        pt_copy(far, h).start()

    def sum_of(q, h):
        return mine[q, rows(h)].astype(jnp.float32) + theirs[q, rows(h)].astype(jnp.float32)

    def rs_copy(d, step, h, src):
        return pltpu.make_async_remote_copy(
            src_ref=src,
            dst_ref=ring_in.at[d, step - 1, h],
            send_sem=rs_send_sem.at[d, step - 1, h],
            recv_sem=rs_recv_sem.at[d, step - 1, h],
            device_id={"ctx": neighbour[d]},
        )

    def rs_step(d, step, k):
        h = order(d)[k]
        sign = 1 - 2 * d
        q = chip(sign * (far + 1 - step))
        if step == 1 or (step == 2 and k == 1):
            mine[q, rows(h)] = sum_of(q, h).astype(jnp.bfloat16)
            src = mine.at[q, rows(h)]
        else:
            src = ring_in.at[d, step - 2, h]
            rs_copy(d, step - 1, h, src).wait_recv()
            ring_in[d, step - 2, h] = (
                ring_in[d, step - 2, h].astype(jnp.float32) + sum_of(q, h)
            ).astype(jnp.bfloat16)
        rs_copy(d, step, h, src).start()

    for offset in range(chips):
        if offset != far:
            y_copy(offset).wait_recv()
    for d in range(2):
        rs_step(d, 2, 1)
    compute(far)
    y_copy(far).wait_recv()
    sends = [(1, 0)]
    for step in range(2, far + 1):
        if step < far:
            sends += [(step + 1, 1)]
        sends += [(step, 0)]
    for step, k in sends:
        for d in range(2):
            rs_step(d, step, k)
    for h in range(2):
        total = hidden[rows(h)] + sum_of(pos, h)
        for d in range(2):
            rs_copy(d, far, h, ring_in.at[d, far - 1, h]).wait_recv()
            total = total + ring_in[d, far - 1, h].astype(jnp.float32)
        out[rows(h)] = total.astype(jnp.bfloat16)

    for d in range(2):
        for step in range(1, far + 1):
            for k in range(2):
                h = order(d)[k]
                if step < far or k == 0:
                    ag_copy(d, step, h).wait_send()
                if step > 1 or k == 0:
                    rs_copy(d, step, h, ring_in.at[d, step - 1, h]).wait_send()
    for offset in range(chips):
        for h in range(2):
            pt_copy(offset, h).wait_send()
        y_copy(offset).wait_send()


    for d in range(2):
        for step in range(1, far + 1):
            for k in range(2):
                if step < far or k == 0:
                    wg_copy(d, step, order(d)[k]).wait_send()
    for offset in range(chips):
        if offset > 0:
            wx_copy(offset).wait_send()
        for kind in range(3):
            wp_copy(offset, kind).wait_send()


def write_kernel(a, b, a_out, b_out, sem):
    copies = [
        pltpu.make_async_copy(x, y, sem.at[k]) for k, (x, y) in enumerate(((a, a_out), (b, b_out)))
    ]
    for copy in copies:
        copy.start()
    for copy in copies:
        copy.wait()


def layer_ring(
    queries,
    keys,
    values,
    block_ids,
    out_weight,
    summary_gain,
    norm_gain,
    routes,
    route_scores,
    expert_gate,
    expert_up,
    expert_down,
    n,
    cap,
):
    tokens, width = queries.shape
    ff = expert_gate.shape[-1]
    chips = n // 2
    far = chips // 2
    vmem = pl.BlockSpec(memory_space=pltpu.VMEM)
    hbm = pl.BlockSpec(memory_space=pl.ANY)
    dma = pltpu.SemaphoreType.DMA
    bf16, f32 = jnp.bfloat16, jnp.float32
    result = jax.ShapeDtypeStruct((tokens, width), bf16)
    pair = pl.pallas_call(
        functools.partial(layer_kernel, n, cap),
        out_shape=(result, result),
        in_specs=[vmem] * 9 + [hbm] * 3,
        out_specs=(vmem, vmem),
        scratch_shapes=[
            pltpu.VMEM((tokens, width), bf16),
            pltpu.VMEM((tokens, width), f32),
            pltpu.VMEM((tokens, width), bf16),
            pltpu.VMEM((chips, 2 * out_weight.shape[0], width), bf16),
            pltpu.VMEM((2 * NB, KVH * HD), bf16),
            pltpu.VMEM((n, 2 * NB, KVH * HD), bf16),
            pltpu.VMEM((n, 8, tokens), f32),
            pltpu.VMEM((width, ff), bf16),
            pltpu.VMEM((width, ff), bf16),
            pltpu.VMEM((ff, width), bf16),
            pltpu.VMEM((chips, 2, tokens, width), bf16),
            pltpu.VMEM((n, 8, tokens), f32),
            pltpu.VMEM((2 * cap, width), bf16),
            pltpu.VMEM((2 * cap, ff), bf16),
            pltpu.VMEM((2, cap, tokens), bf16),
            pltpu.VMEM((2, cap, 128), f32),
            pltpu.VMEM((chips, tokens, width), bf16),
            pltpu.VMEM((chips, tokens, width), bf16),
            pltpu.VMEM((chips, tokens, width), bf16),
            pltpu.VMEM((2, far, 2, tokens // 2, width), bf16),
            dma((3,)),
            dma((n,)),
            dma((n,)),
            dma((2, far, 2)),
            dma((2, far, 2)),
            dma((chips,)),
            dma((chips,)),
            dma((chips, 3)),
            dma((chips, 3)),
            dma((n,)),
            dma((n,)),
            dma((2, far, 2)),
            dma((2, far, 2)),
            dma((chips, 2)),
            dma((chips, 2)),
            dma((chips,)),
            dma((chips,)),
            dma((2, far, 2)),
            dma((2, far, 2)),
        ],
        compiler_params=pltpu.CompilerParams(
            collective_id=1, has_side_effects=True, vmem_limit_bytes=62 * 2**20
        ),
    )(
        queries,
        keys,
        values,
        block_ids[None, :],
        out_weight,
        summary_gain[None, :],
        norm_gain[None, :],
        routes.T,
        route_scores.T,
        expert_gate[0],
        expert_up[0],
        expert_down[0],
    )
    return pl.pallas_call(
        write_kernel,
        out_shape=(result, result),
        in_specs=[vmem] * 2,
        out_specs=(hbm, hbm),
        scratch_shapes=[dma((2,))],
    )(*pair)


def body(
    queries,
    keys,
    values,
    block_ids,
    out_weight,
    summary_gain,
    norm_gain,
    routes,
    route_scores,
    expert_gate,
    expert_up,
    expert_down,
):
    tokens_here = queries.shape[0]
    combine = route_scores / jnp.sum(route_scores, axis=-1, keepdims=True)
    experts_all = EXP_DEV * lax.axis_size("ctx")
    capacity = max(2, 5 * tokens_here * TOP // (4 * experts_all))
    chips = experts_all // 2
    fits = experts_all * tokens_here * D * 2 <= RING_BYTES
    if fits and chips % 4 == 0 and lax.axis_size("groups") == 2:
        return layer_ring(
            queries,
            keys,
            values,
            block_ids,
            out_weight,
            summary_gain,
            norm_gain,
            routes,
            route_scores,
            expert_gate,
            expert_up,
            expert_down,
            experts_all,
            -(-capacity // 16) * 16,
        )
    group = HQ // KVH
    scale = 1.0 / math.sqrt(HD)
    member = block_ids[None, :] == jnp.arange(NB, dtype=jnp.int32)[:, None]
    count = jnp.sum(member.astype(jnp.float32), axis=-1)
    indicator = member.astype(jnp.bfloat16)
    kmean = jnp.dot(indicator, keys, preferred_element_type=jnp.float32) / count[:, None]
    vmean = jnp.dot(indicator, values, preferred_element_type=jnp.float32) / count[:, None]
    summary_keys = (
        (normalize(kmean.reshape(NB, KVH, HD)) * summary_gain)
        .astype(jnp.bfloat16)
        .reshape(NB, KVH * HD)
    )
    summary_values = (
        normalize(vmean.reshape(NB, KVH, HD)).astype(jnp.bfloat16).reshape(NB, KVH * HD)
    )
    summaries = lax.all_gather(
        jnp.concatenate([summary_keys, summary_values], axis=1), "ctx", axis=0, tiled=True
    )
    all_keys, all_values = summaries[:, : KVH * HD], summaries[:, KVH * HD :]
    index = lax.axis_index("ctx")
    query = queries.reshape(tokens_here, KVH, group, HD)
    key_loc = keys.reshape(tokens_here, KVH, HD)
    remote_keys = all_keys.reshape(-1, KVH, HD)
    causal = jnp.arange(tokens_here)[:, None] >= jnp.arange(tokens_here)[None, :]
    owner = jnp.arange(remote_keys.shape[0], dtype=jnp.int32) // NB
    local = jnp.einsum("tkgd,skd->kgts", query, key_loc, preferred_element_type=jnp.float32) * scale
    local = jnp.where(causal[None, None], local, -jnp.inf)
    remote = (
        jnp.einsum("tkgd,skd->kgts", query, remote_keys, preferred_element_type=jnp.float32) * scale
    )
    remote = jnp.where((owner < index)[None, None, None, :], remote, -jnp.inf)
    scores = jnp.concatenate([local, remote], axis=-1)
    top = jnp.max(scores, axis=-1, keepdims=True)
    expo = jnp.exp(scores - top)
    weights = (expo / jnp.sum(expo, axis=-1, keepdims=True)).astype(jnp.bfloat16)
    every_value = jnp.concatenate(
        [values.reshape(tokens_here, KVH, HD), all_values.reshape(-1, KVH, HD)], axis=0
    )
    attended = jnp.einsum(
        "kgts,skd->tkgd", weights, every_value, preferred_element_type=jnp.float32
    )
    attended = attended.reshape(tokens_here, HQ * HD).astype(jnp.bfloat16)
    hidden = jnp.dot(
        attended,
        lax.all_gather(out_weight, "ctx", axis=0, tiled=True),
        preferred_element_type=jnp.float32,
    )
    normed = (normalize(hidden) * norm_gain).astype(jnp.bfloat16)
    flat_routes = routes.reshape(-1)
    hits = (flat_routes[:, None] == jnp.arange(experts_all, dtype=jnp.int32)[None, :]).astype(
        jnp.int32
    )
    slot = jnp.sum(hits * (jnp.cumsum(hits, axis=0) - 1), axis=-1)
    target = flat_routes * capacity + slot
    source = jnp.arange(tokens_here * TOP, dtype=jnp.int32) // TOP
    outgoing = jnp.zeros((experts_all * capacity, D), jnp.bfloat16).at[target].set(normed[source])
    outgoing = outgoing.reshape(experts_all, capacity, D)
    arrived = lax.all_to_all(outgoing, "ctx", split_axis=0, concat_axis=0, tiled=True)
    senders = arrived.shape[0] // EXP_DEV
    width = arrived.shape[1]
    inputs = (
        arrived.reshape(senders, EXP_DEV, width, D)
        .transpose(1, 0, 2, 3)
        .reshape(EXP_DEV, senders * width, D)
    )
    gate = jnp.einsum("erd,edf->erf", inputs, expert_gate, preferred_element_type=jnp.float32)
    upper = jnp.einsum("erd,edf->erf", inputs, expert_up, preferred_element_type=jnp.float32)
    act = (jax.nn.silu(gate) * upper).astype(jnp.bfloat16)
    result = jnp.einsum(
        "erf,efd->erd", act, expert_down, preferred_element_type=jnp.float32
    ).astype(jnp.bfloat16)
    result = (
        result.reshape(EXP_DEV, senders, width, D)
        .transpose(1, 0, 2, 3)
        .reshape(senders * EXP_DEV, width, D)
    )
    returned = lax.all_to_all(result, "ctx", split_axis=0, concat_axis=0, tiled=True)
    returned = returned.reshape(experts_all * capacity, D)
    picked = jnp.take(returned, target, axis=0).reshape(tokens_here, TOP, D)
    blended = jnp.sum(combine[:, :, None] * picked.astype(jnp.float32), axis=1)
    return (hidden.astype(jnp.bfloat16), (hidden + blended).astype(jnp.bfloat16))


def solution(mesh):
    in_specs = (
        P(("groups", "ctx"), None),
        P(("groups", "ctx"), None),
        P(("groups", "ctx"), None),
        P(("groups", "ctx")),
        P("ctx", None),
        P(),
        P(),
        P(("groups", "ctx"), None),
        P(("groups", "ctx"), None),
        P("ctx", None, None),
        P("ctx", None, None),
        P("ctx", None, None),
    )
    out_specs = (P(("groups", "ctx"), None), P(("groups", "ctx"), None))
    return jax.shard_map(body, mesh=mesh, in_specs=in_specs, out_specs=out_specs, check_vma=False)
```

```python
import functools
import math

import jax
import jax.numpy as jnp
from jax import lax
from jax.experimental import pallas as pl
from jax.experimental.pallas import tpu as pltpu
from jax.sharding import PartitionSpec as P

D = 2048
HQ = 16
KVH = 4
HD = 128
TOP = 8
EXP_DEV = 1
NB = 4


def normalize(x):
    return x * lax.rsqrt(jnp.mean(x * x, axis=-1, keepdims=True) + 1e-06)


RING_BYTES = 16 * 2**20


def chip_at(position, chips):
    depth = chips // 2
    y = position // depth
    return (position * (1 - y) + (chips - 1 - position) * y) * 2 + y


def layer_kernel(
    n,
    cap,
    queries,
    keys,
    values,
    blocks,
    weight_own,
    key_gain,
    norm_gain,
    routes,
    route_scores,
    gate_hbm,
    up_hbm,
    down_hbm,
    projected,
    out,
    normed,
    hidden,
    att,
    wg,
    sums_own,
    sums,
    share,
    gate_w,
    up_w,
    down_w,
    tok,
    wbuf,
    rows_in,
    act,
    place,
    comb,
    mine,
    outgo,
    theirs,
    ring_in,
    load_sem,
    s_send,
    s_recv,
    wg_send,
    wg_recv,
    wx_send,
    wx_recv,
    wp_send,
    wp_recv,
    w_send,
    w_recv,
    ag_send,
    ag_recv,
    pt_send,
    pt_recv,
    y_send,
    y_recv,
    rs_send_sem,
    rs_recv_sem,
):
    tokens = normed.shape[0]
    half = tokens // 2
    width = normed.shape[1]
    ff = gate_w.shape[1]
    chips = n // 2
    far = chips // 2
    me = lax.axis_index("ctx")
    core = me % 2
    y = (me // 2) % 2
    z = me // 4
    pos = z * (1 - y) + (chips - 1 - z) * y
    partner = me + 1 - 2 * core
    ahead = chip_at((pos + 1) % chips, chips) * 2 + core
    behind = chip_at((pos + chips - 1) % chips, chips) * 2 + core
    neighbour = (ahead, behind)

    loads = [
        pltpu.make_async_copy(a, b, load_sem.at[k])
        for k, (a, b) in enumerate(((gate_hbm, gate_w), (up_hbm, up_w), (down_hbm, down_w)))
    ]
    for load in loads:
        load.start()

    barrier = pltpu.get_barrier_semaphore()
    across = 1 - lax.axis_index("groups")

    def greet(k, _):
        pl.semaphore_signal(barrier, inc=1, device_id={"ctx": (me + k) % n})
        return 0

    lax.fori_loop(1, n, greet, 0)
    pl.semaphore_signal(barrier, inc=1, device_id={"groups": across})

    def mean_of(ref):
        shape = (2 * NB, tokens)
        ids = jnp.broadcast_to(blocks[...], shape)
        member = jnp.where(ids == lax.broadcasted_iota(jnp.int32, shape, 0) % NB, 1.0, 0.0)
        count = jnp.sum(member, axis=1, keepdims=True)
        return (
            jnp.dot(member.astype(jnp.bfloat16), ref[...], preferred_element_type=jnp.float32)
            / count
        )

    kmean, vmean = mean_of(keys), mean_of(values)
    upper = lax.broadcasted_iota(jnp.int32, (2 * NB, HD), 0) < NB
    for g in range(KVH):
        cols = slice(g * HD, (g + 1) * HD)
        sums_own[:, cols] = jnp.where(
            upper, normalize(kmean[:, cols]) * key_gain[...], normalize(vmean[:, cols])
        ).astype(jnp.bfloat16)
    pl.semaphore_wait(barrier, n)

    def s_copy(k):
        target = (me + k) % n
        return pltpu.make_async_remote_copy(
            src_ref=sums_own,
            dst_ref=sums.at[me],
            send_sem=s_send.at[k],
            recv_sem=s_recv.at[k],
            device_id={"ctx": target},
        )

    def s_start(k, _):
        s_copy(k).start()
        return 0

    def s_wait(k, _):
        s_copy(k).wait()
        return 0

    lax.fori_loop(1, n, s_start, 0)
    sums[me] = sums_own[...]

    def rows(h):
        return pl.ds(h * half, half)

    def chip(offset):
        return (pos + offset + chips) % chips

    def ag_copy(d, step, h):
        sign = 1 - 2 * d
        q = chip(-sign * (step - 1))
        src = normed.at[rows(h)] if step == 1 else tok.at[q, core, rows(h)]
        return pltpu.make_async_remote_copy(
            src_ref=src,
            dst_ref=tok.at[q, core, rows(h)],
            send_sem=ag_send.at[d, step - 1, h],
            recv_sem=ag_recv.at[d, step - 1, h],
            device_id={"ctx": neighbour[d]},
        )

    def pt_copy(offset, h):
        q = chip(offset)
        src = normed.at[rows(h)] if offset == 0 else tok.at[q, core, rows(h)]
        return pltpu.make_async_remote_copy(
            src_ref=src,
            dst_ref=tok.at[q, core, rows(h)],
            send_sem=pt_send.at[offset % chips, h],
            recv_sem=pt_recv.at[offset % chips, h],
            device_id={"ctx": partner},
        )

    def order(d):
        return (0, 1) if d == 0 else (1, 0)

    wrows = weight_own.shape[0]
    side = wrows // 4
    middle = wrows - 2 * side
    group = 1 - across
    mine_side = group * (side + middle)
    other_side = across * (side + middle)

    def w_rows(kind):
        if kind == 0:
            return mine_side, side
        if kind == 1:
            return side, middle
        return other_side, side

    def w_at(q, kind):
        start, size = w_rows(kind)
        return wg.at[q, pl.ds(core * wrows + start, size)]

    def w_first(kind):
        start, size = w_rows(kind)
        return weight_own.at[pl.ds(start, size)]

    def wg_copy(d, step, h):
        sign = 1 - 2 * d
        q = chip(-sign * (step - 1))
        return pltpu.make_async_remote_copy(
            src_ref=w_first(h) if step == 1 else w_at(q, h),
            dst_ref=w_at(q, h),
            send_sem=wg_send.at[d, step - 1, h],
            recv_sem=wg_recv.at[d, step - 1, h],
            device_id={"ctx": neighbour[d]},
        )

    def wx_copy(offset):
        q = chip(offset)
        return pltpu.make_async_remote_copy(
            src_ref=w_at(q, 0),
            dst_ref=w_at(q, 0),
            send_sem=wx_send.at[offset % chips],
            recv_sem=wx_recv.at[offset % chips],
            device_id={"groups": across},
        )

    def wp_copy(offset, kind):
        q = chip(offset)
        return pltpu.make_async_remote_copy(
            src_ref=w_first(kind) if offset == 0 else w_at(q, kind),
            dst_ref=w_at(q, kind),
            send_sem=wp_send.at[offset % chips, kind],
            recv_sem=wp_recv.at[offset % chips, kind],
            device_id={"ctx": partner},
        )

    for k in range(2):
        for d in range(2):
            wg_copy(d, 1, order(d)[k]).start()
    for kind in range(3):
        wp_copy(0, kind).start()
    wg[pos, pl.ds(pl.multiple_of(core * wrows, wrows), wrows)] = weight_own[...]

    def w_copy(k):
        target = (me + k) % n
        return pltpu.make_async_remote_copy(
            src_ref=share.at[target],
            dst_ref=wbuf.at[pos * 2 + core],
            send_sem=w_send.at[k],
            recv_sem=w_recv.at[k],
            device_id={"ctx": target},
        )

    def w_start(k, _):
        w_copy(k).start()
        return 0

    def w_wait(k, _):
        w_copy(k).wait()
        return 0

    chosen_scores = route_scores[...]
    combine = chosen_scores / jnp.sum(chosen_scores, axis=0, keepdims=True)
    expert = lax.broadcasted_iota(jnp.int32, (n, tokens), 0)
    table_of = jnp.zeros((n, tokens), jnp.float32)
    for c in range(TOP):
        table_of = table_of + jnp.where(routes[c : c + 1] == expert, combine[c : c + 1], 0.0)
    for e in range(n):
        share[e] = jnp.broadcast_to(table_of[e : e + 1], (8, tokens))
    lax.fori_loop(1, n, w_start, 0)
    wbuf[pos * 2 + core] = share[me]
    lax.fori_loop(1, n, s_wait, 0)

    many = HQ // KVH
    scale = 1.0 / math.sqrt(HD)
    tall = (many * tokens, tokens)
    causal = lax.broadcasted_iota(jnp.int32, tall, 0) % tokens >= lax.broadcasted_iota(
        jnp.int32, tall, 1
    )
    far_shape = (many * tokens, n * 2 * NB)
    entry = lax.broadcasted_iota(jnp.int32, far_shape, 1)
    seen = (entry % (2 * NB) < NB) & (entry // (2 * NB) < me)
    contract_last = (((1,), (1,)), ((), ()))

    def attend(g):
        cols = slice(g * HD, (g + 1) * HD)
        heads = [slice((g * many + i) * HD, (g * many + i + 1) * HD) for i in range(many)]
        q = jnp.concatenate([queries[:, c] for c in heads], axis=0)
        table = sums[:, :, cols].astype(jnp.float32).reshape(n * 2 * NB, HD)
        shifted = jnp.concatenate([table[NB:], table[:NB]], axis=0).astype(jnp.bfloat16)
        table = table.astype(jnp.bfloat16)
        near = (
            lax.dot_general(q, keys[:, cols], contract_last, preferred_element_type=jnp.float32)
            * scale
        )
        near = jnp.where(causal, near, -jnp.inf)
        remote = lax.dot_general(q, table, contract_last, preferred_element_type=jnp.float32) * scale
        remote = jnp.where(seen, remote, -jnp.inf)
        top = jnp.maximum(
            jnp.max(near, axis=1, keepdims=True), jnp.max(remote, axis=1, keepdims=True)
        )
        near, remote = jnp.exp(near - top), jnp.exp(remote - top)
        total = jnp.sum(near, axis=1, keepdims=True) + jnp.sum(remote, axis=1, keepdims=True)
        near, remote = (near / total).astype(jnp.bfloat16), (remote / total).astype(jnp.bfloat16)
        result = jnp.dot(
            near, values[:, cols], preferred_element_type=jnp.float32
        ) + jnp.dot(remote, shifted, preferred_element_type=jnp.float32)
        result = result.astype(jnp.bfloat16)
        for i, c in enumerate(heads):
            att[:, c] = result[i * tokens : (i + 1) * tokens]

    def project(offset):
        q = chip(offset)
        for kind in range(3):
            wp_copy(offset, kind).wait_recv()
        place_at = pl.multiple_of(chip_at(q, chips) * 2 * wrows, 2 * wrows)
        left = att[:, pl.ds(place_at, 2 * wrows)]

        def tile(k, _):
            cols = pl.ds(pl.multiple_of(k * 512, 512), 512)
            part = jnp.dot(left, wg[q, :, cols], preferred_element_type=jnp.float32)
            hidden[:, cols] = part if offset == 0 else hidden[:, cols] + part
            return 0

        lax.fori_loop(0, width // 512, tile, 0)

    def w_step(step, k):
        for d in range(2):
            h = order(d)[k]
            sign = 1 - 2 * d
            wg_copy(d, step, h).wait_recv()
            if step + 1 < far or (step + 1 == far and k == 0):
                wg_copy(d, step + 1, h).start()
            if h == 0:
                wx_copy(-sign * step).start()
            wp_copy(-sign * step, h).start()

    def x_step(offset):
        wx_copy(offset).wait_recv()
        wp_copy(offset, 2).start()

    attend(0)
    attend(1)
    w_step(1, 0)
    attend(2)
    w_step(1, 1)
    attend(3)
    for step in range(2, far):
        w_step(step, 0)
        x_step(1 - step)
        x_step(step - 1)
        if step == 2:
            project(0)
        else:
            project(2 - step)
        w_step(step, 1)
        if step > 2:
            project(step - 2)
    w_step(far, 0)
    x_step(1 - far)
    x_step(far - 1)
    project(2 - far)
    project(far - 2)
    x_step(far)
    project(1 - far)
    project(far - 1)
    project(far)
    for h in range(2):
        hid = hidden[rows(h)]
        projected[rows(h)] = hid.astype(jnp.bfloat16)
        tidy = (normalize(hid) * norm_gain[...]).astype(jnp.bfloat16)
        normed[rows(h)] = tidy
        tok[pos, core, rows(h)] = tidy

    for k in range(2):
        for d in range(2):
            ag_copy(d, 1, order(d)[k]).start()
    for h in range(2):
        pt_copy(0, h).start()

    lax.fori_loop(1, n, w_wait, 0)
    for load in loads:
        load.wait()

    def y_copy(offset):
        q = chip(offset)
        return pltpu.make_async_remote_copy(
            src_ref=outgo.at[q],
            dst_ref=theirs.at[q],
            send_sem=y_send.at[offset % chips],
            recv_sem=y_recv.at[offset % chips],
            device_id={"ctx": partner},
        )

    def compute(offset):
        q = chip(offset)
        for h in range(2):
            pt_copy(offset, h).wait_recv()
        earlier = lax.broadcasted_iota(jnp.int32, (tokens, tokens), 0) < lax.broadcasted_iota(
            jnp.int32, (tokens, tokens), 1
        )
        earlier = jnp.where(earlier, 1.0, 0.0).astype(jnp.bfloat16)
        line = lax.broadcasted_iota(jnp.int32, (cap, tokens), 0).astype(jnp.float32)
        for rel in range(2):
            side = (core + rel) % 2
            weight = wbuf[q * 2 + side]
            chosen = jnp.where(weight > 0.0, 1.0, 0.0)
            slot = jnp.dot(chosen.astype(jnp.bfloat16), earlier, preferred_element_type=jnp.float32)
            slot = jnp.where(weight > 0.0, slot, -1.0)
            hit = jnp.broadcast_to(slot[0:1], (cap, tokens)) == line
            pick = jnp.where(hit, 1.0, 0.0).astype(jnp.bfloat16)
            place[rel] = pick
            scaled = jnp.where(hit, jnp.broadcast_to(weight[0:1], (cap, tokens)), 0.0)
            comb[rel] = jnp.broadcast_to(jnp.sum(scaled, axis=1, keepdims=True), (cap, 128))
            for c in range(0, width, 512):
                rows_in[rel * cap : (rel + 1) * cap, c : c + 512] = jnp.dot(
                    pick, tok[q, side, :, c : c + 512], preferred_element_type=jnp.float32
                ).astype(jnp.bfloat16)

        def in_tile(k, _):
            cols = pl.ds(pl.multiple_of(k * 256, 256), 256)
            x = rows_in[...]
            g = jnp.dot(x, gate_w[:, cols], preferred_element_type=jnp.float32)
            u = jnp.dot(x, up_w[:, cols], preferred_element_type=jnp.float32)
            act[:, cols] = (g / (1.0 + jnp.exp(-g)) * u).astype(jnp.bfloat16)
            return 0

        lax.fori_loop(0, ff // 256, in_tile, 0)

        def out_tile(k, _):
            cols = pl.ds(pl.multiple_of(k * 512, 512), 512)
            r = jnp.dot(act[...], down_w[:, cols], preferred_element_type=jnp.float32)
            r = r.astype(jnp.bfloat16).astype(jnp.float32)
            for rel, dest in ((0, mine), (1, outgo)):
                part = r[rel * cap : (rel + 1) * cap] * comb[rel][:, 0:1]
                dest[q, :, cols] = lax.dot_general(
                    place[rel],
                    part.astype(jnp.bfloat16),
                    (((0,), (0,)), ((), ())),
                    preferred_element_type=jnp.float32,
                ).astype(jnp.bfloat16)
            return 0

        lax.fori_loop(0, width // 512, out_tile, 0)
        y_copy(offset).start()

    for step in range(1, far):
        for k in range(2):
            for d in range(2):
                h = order(d)[k]
                sign = 1 - 2 * d
                ag_copy(d, step, h).wait_recv()
                if step + 1 < far or k == 0:
                    ag_copy(d, step + 1, h).start()
                pt_copy(-sign * step, h).start()
            if step == 1:
                if k == 0:
                    compute(0)
            else:
                compute((step - 1) * (2 * k - 1))
    compute(1 - far)
    compute(far - 1)
    for d in range(2):
        h = order(d)[0]
        ag_copy(d, far, h).wait_recv()
        pt_copy(far, h).start()

    def sum_of(q, h):
        return mine[q, rows(h)].astype(jnp.float32) + theirs[q, rows(h)].astype(jnp.float32)

    def rs_copy(d, step, h, src):
        return pltpu.make_async_remote_copy(
            src_ref=src,
            dst_ref=ring_in.at[d, step - 1, h],
            send_sem=rs_send_sem.at[d, step - 1, h],
            recv_sem=rs_recv_sem.at[d, step - 1, h],
            device_id={"ctx": neighbour[d]},
        )

    def rs_step(d, step, k):
        h = order(d)[k]
        sign = 1 - 2 * d
        q = chip(sign * (far + 1 - step))
        if step == 1 or (step == 2 and k == 1):
            mine[q, rows(h)] = sum_of(q, h).astype(jnp.bfloat16)
            src = mine.at[q, rows(h)]
        else:
            src = ring_in.at[d, step - 2, h]
            rs_copy(d, step - 1, h, src).wait_recv()
            ring_in[d, step - 2, h] = (
                ring_in[d, step - 2, h].astype(jnp.float32) + sum_of(q, h)
            ).astype(jnp.bfloat16)
        rs_copy(d, step, h, src).start()

    for offset in range(chips):
        if offset != far:
            y_copy(offset).wait_recv()
    for d in range(2):
        rs_step(d, 2, 1)
    compute(far)
    y_copy(far).wait_recv()
    sends = [(1, 0)]
    for step in range(2, far + 1):
        if step < far:
            sends += [(step + 1, 1)]
        sends += [(step, 0)]
    for step, k in sends:
        for d in range(2):
            rs_step(d, step, k)
    for h in range(2):
        total = hidden[rows(h)] + sum_of(pos, h)
        for d in range(2):
            rs_copy(d, far, h, ring_in.at[d, far - 1, h]).wait_recv()
            total = total + ring_in[d, far - 1, h].astype(jnp.float32)
        out[rows(h)] = total.astype(jnp.bfloat16)

    for d in range(2):
        for step in range(1, far + 1):
            for k in range(2):
                h = order(d)[k]
                if step < far or k == 0:
                    ag_copy(d, step, h).wait_send()
                if step > 1 or k == 0:
                    rs_copy(d, step, h, ring_in.at[d, step - 1, h]).wait_send()
    for offset in range(chips):
        for h in range(2):
            pt_copy(offset, h).wait_send()
        y_copy(offset).wait_send()


    for d in range(2):
        for step in range(1, far + 1):
            for k in range(2):
                if step < far or k == 0:
                    wg_copy(d, step, order(d)[k]).wait_send()
    for offset in range(chips):
        if offset > 0:
            wx_copy(offset).wait_send()
        for kind in range(3):
            wp_copy(offset, kind).wait_send()


def write_kernel(a, b, a_out, b_out, sem):
    copies = [
        pltpu.make_async_copy(x, y, sem.at[k]) for k, (x, y) in enumerate(((a, a_out), (b, b_out)))
    ]
    for copy in copies:
        copy.start()
    for copy in copies:
        copy.wait()


def layer_ring(
    queries,
    keys,
    values,
    block_ids,
    out_weight,
    summary_gain,
    norm_gain,
    routes,
    route_scores,
    expert_gate,
    expert_up,
    expert_down,
    n,
    cap,
):
    tokens, width = queries.shape
    ff = expert_gate.shape[-1]
    chips = n // 2
    far = chips // 2
    vmem = pl.BlockSpec(memory_space=pltpu.VMEM)
    hbm = pl.BlockSpec(memory_space=pl.ANY)
    dma = pltpu.SemaphoreType.DMA
    bf16, f32 = jnp.bfloat16, jnp.float32
    result = jax.ShapeDtypeStruct((tokens, width), bf16)
    pair = pl.pallas_call(
        functools.partial(layer_kernel, n, cap),
        out_shape=(result, result),
        in_specs=[vmem] * 9 + [hbm] * 3,
        out_specs=(vmem, vmem),
        scratch_shapes=[
            pltpu.VMEM((tokens, width), bf16),
            pltpu.VMEM((tokens, width), f32),
            pltpu.VMEM((tokens, width), bf16),
            pltpu.VMEM((chips, 2 * out_weight.shape[0], width), bf16),
            pltpu.VMEM((2 * NB, KVH * HD), bf16),
            pltpu.VMEM((n, 2 * NB, KVH * HD), bf16),
            pltpu.VMEM((n, 8, tokens), f32),
            pltpu.VMEM((width, ff), bf16),
            pltpu.VMEM((width, ff), bf16),
            pltpu.VMEM((ff, width), bf16),
            pltpu.VMEM((chips, 2, tokens, width), bf16),
            pltpu.VMEM((n, 8, tokens), f32),
            pltpu.VMEM((2 * cap, width), bf16),
            pltpu.VMEM((2 * cap, ff), bf16),
            pltpu.VMEM((2, cap, tokens), bf16),
            pltpu.VMEM((2, cap, 128), f32),
            pltpu.VMEM((chips, tokens, width), bf16),
            pltpu.VMEM((chips, tokens, width), bf16),
            pltpu.VMEM((chips, tokens, width), bf16),
            pltpu.VMEM((2, far, 2, tokens // 2, width), bf16),
            dma((3,)),
            dma((n,)),
            dma((n,)),
            dma((2, far, 2)),
            dma((2, far, 2)),
            dma((chips,)),
            dma((chips,)),
            dma((chips, 3)),
            dma((chips, 3)),
            dma((n,)),
            dma((n,)),
            dma((2, far, 2)),
            dma((2, far, 2)),
            dma((chips, 2)),
            dma((chips, 2)),
            dma((chips,)),
            dma((chips,)),
            dma((2, far, 2)),
            dma((2, far, 2)),
        ],
        compiler_params=pltpu.CompilerParams(
            collective_id=1, has_side_effects=True, vmem_limit_bytes=62 * 2**20
        ),
    )(
        queries,
        keys,
        values,
        block_ids[None, :],
        out_weight,
        summary_gain[None, :],
        norm_gain[None, :],
        routes.T,
        route_scores.T,
        expert_gate[0],
        expert_up[0],
        expert_down[0],
    )
    return pl.pallas_call(
        write_kernel,
        out_shape=(result, result),
        in_specs=[vmem] * 2,
        out_specs=(hbm, hbm),
        scratch_shapes=[dma((2,))],
    )(*pair)


def body(
    queries,
    keys,
    values,
    block_ids,
    out_weight,
    summary_gain,
    norm_gain,
    routes,
    route_scores,
    expert_gate,
    expert_up,
    expert_down,
):
    tokens_here = queries.shape[0]
    combine = route_scores / jnp.sum(route_scores, axis=-1, keepdims=True)
    experts_all = EXP_DEV * lax.axis_size("ctx")
    capacity = max(2, 5 * tokens_here * TOP // (4 * experts_all))
    chips = experts_all // 2
    fits = experts_all * tokens_here * D * 2 <= RING_BYTES
    if fits and chips % 4 == 0 and lax.axis_size("groups") == 2:
        return layer_ring(
            queries,
            keys,
            values,
            block_ids,
            out_weight,
            summary_gain,
            norm_gain,
            routes,
            route_scores,
            expert_gate,
            expert_up,
            expert_down,
            experts_all,
            -(-capacity // 16) * 16,
        )
    group = HQ // KVH
    scale = 1.0 / math.sqrt(HD)
    member = block_ids[None, :] == jnp.arange(NB, dtype=jnp.int32)[:, None]
    count = jnp.sum(member.astype(jnp.float32), axis=-1)
    indicator = member.astype(jnp.bfloat16)
    kmean = jnp.dot(indicator, keys, preferred_element_type=jnp.float32) / count[:, None]
    vmean = jnp.dot(indicator, values, preferred_element_type=jnp.float32) / count[:, None]
    summary_keys = (
        (normalize(kmean.reshape(NB, KVH, HD)) * summary_gain)
        .astype(jnp.bfloat16)
        .reshape(NB, KVH * HD)
    )
    summary_values = (
        normalize(vmean.reshape(NB, KVH, HD)).astype(jnp.bfloat16).reshape(NB, KVH * HD)
    )
    summaries = lax.all_gather(
        jnp.concatenate([summary_keys, summary_values], axis=1), "ctx", axis=0, tiled=True
    )
    all_keys, all_values = summaries[:, : KVH * HD], summaries[:, KVH * HD :]
    index = lax.axis_index("ctx")
    query = queries.reshape(tokens_here, KVH, group, HD)
    key_loc = keys.reshape(tokens_here, KVH, HD)
    remote_keys = all_keys.reshape(-1, KVH, HD)
    causal = jnp.arange(tokens_here)[:, None] >= jnp.arange(tokens_here)[None, :]
    owner = jnp.arange(remote_keys.shape[0], dtype=jnp.int32) // NB
    local = jnp.einsum("tkgd,skd->kgts", query, key_loc, preferred_element_type=jnp.float32) * scale
    local = jnp.where(causal[None, None], local, -jnp.inf)
    remote = (
        jnp.einsum("tkgd,skd->kgts", query, remote_keys, preferred_element_type=jnp.float32) * scale
    )
    remote = jnp.where((owner < index)[None, None, None, :], remote, -jnp.inf)
    scores = jnp.concatenate([local, remote], axis=-1)
    top = jnp.max(scores, axis=-1, keepdims=True)
    expo = jnp.exp(scores - top)
    weights = (expo / jnp.sum(expo, axis=-1, keepdims=True)).astype(jnp.bfloat16)
    every_value = jnp.concatenate(
        [values.reshape(tokens_here, KVH, HD), all_values.reshape(-1, KVH, HD)], axis=0
    )
    attended = jnp.einsum(
        "kgts,skd->tkgd", weights, every_value, preferred_element_type=jnp.float32
    )
    attended = attended.reshape(tokens_here, HQ * HD).astype(jnp.bfloat16)
    hidden = jnp.dot(
        attended,
        lax.all_gather(out_weight, "ctx", axis=0, tiled=True),
        preferred_element_type=jnp.float32,
    )
    normed = (normalize(hidden) * norm_gain).astype(jnp.bfloat16)
    flat_routes = routes.reshape(-1)
    hits = (flat_routes[:, None] == jnp.arange(experts_all, dtype=jnp.int32)[None, :]).astype(
        jnp.int32
    )
    slot = jnp.sum(hits * (jnp.cumsum(hits, axis=0) - 1), axis=-1)
    target = flat_routes * capacity + slot
    source = jnp.arange(tokens_here * TOP, dtype=jnp.int32) // TOP
    outgoing = jnp.zeros((experts_all * capacity, D), jnp.bfloat16).at[target].set(normed[source])
    outgoing = outgoing.reshape(experts_all, capacity, D)
    arrived = lax.all_to_all(outgoing, "ctx", split_axis=0, concat_axis=0, tiled=True)
    senders = arrived.shape[0] // EXP_DEV
    width = arrived.shape[1]
    inputs = (
        arrived.reshape(senders, EXP_DEV, width, D)
        .transpose(1, 0, 2, 3)
        .reshape(EXP_DEV, senders * width, D)
    )
    gate = jnp.einsum("erd,edf->erf", inputs, expert_gate, preferred_element_type=jnp.float32)
    upper = jnp.einsum("erd,edf->erf", inputs, expert_up, preferred_element_type=jnp.float32)
    act = (jax.nn.silu(gate) * upper).astype(jnp.bfloat16)
    result = jnp.einsum(
        "erf,efd->erd", act, expert_down, preferred_element_type=jnp.float32
    ).astype(jnp.bfloat16)
    result = (
        result.reshape(EXP_DEV, senders, width, D)
        .transpose(1, 0, 2, 3)
        .reshape(senders * EXP_DEV, width, D)
    )
    returned = lax.all_to_all(result, "ctx", split_axis=0, concat_axis=0, tiled=True)
    returned = returned.reshape(experts_all * capacity, D)
    picked = jnp.take(returned, target, axis=0).reshape(tokens_here, TOP, D)
    blended = jnp.sum(combine[:, :, None] * picked.astype(jnp.float32), axis=1)
    return (hidden.astype(jnp.bfloat16), (hidden + blended).astype(jnp.bfloat16))


def solution(mesh):
    in_specs = (
        P(("groups", "ctx"), None),
        P(("groups", "ctx"), None),
        P(("groups", "ctx"), None),
        P(("groups", "ctx")),
        P("ctx", None),
        P(),
        P(),
        P(("groups", "ctx"), None),
        P(("groups", "ctx"), None),
        P("ctx", None, None),
        P("ctx", None, None),
        P("ctx", None, None),
    )
    out_specs = (P(("groups", "ctx"), None), P(("groups", "ctx"), None))
    return jax.shard_map(body, mesh=mesh, in_specs=in_specs, out_specs=out_specs, check_vma=False)
```
